128 devices in a mesh: row: 16 (over z_hi, y, core), col: 8 (over z_lo, x).
Axes of the slice: x: 4, y: 4, z: 4 (z_hi: 2, z_lo: 2; z = z_hi * 2 + z_lo), core: 2. Of those that a mesh axis runs over, the one named last changes fastest.
Arguments:
- at: bfloat16 [32768, 16384], P('row', 'col'), may hold values from -0.09375 to 0.09375
- bmat: bfloat16 [32768, 16384], P('col', 'row'), may hold values from -6 to 6
- mask_a: int32 [512, 256], P('row', 'col'), may hold values 0 or 1
- mask_b: int32 [512, 256], P('col', 'row'), may hold values 0 or 1
- filt: int32 [256, 256], P('col', 'row'), may hold values 0 or 1
- kdist: int32 [512], replicated, may hold values from 0 to 511, as said below
Outputs:
- product_blocks: float32 [16384, 16384], P('col', 'row')
The draws below stay inside these ranges and needn't reach their ends.
Inputs may be any that keep to these rules, and one draw needn't show every extreme that they name: kdist is a permutation; entry k lies in run s = k // 32 and equals p * 32 + s * 2 + j for some panel p and j below 2, each run giving every panel exactly 2 blocks.
All inputs are finite; a program needn't handle non-finite values. No bound on the sum of `mask_a` or of `mask_b` or of `filt` on one device may be relied on, other than what follows from the above.
Results may differ from the reference program's by a relative error of at most 0.0003.
Values may be sent and summed in bfloat16 or wider, within the bound.
No kernel may reach another device: no remote copies, remote signals or barrier semaphores. Data moves between devices by JAX's collectives and lax.ppermute only.
A program may use at most 192 MiB of HBM per device.

```python
import jax
import jax.numpy as jnp
from jax import lax

BS = 64
RB = 16
CB = 16
KB = 32
PANELS = 16
CAP = 2


def draw_kdist(key, part):
    key_list = jax.random.split(jax.random.fold_in(key, 11), PANELS)
    orders = jax.vmap(lambda single: jax.random.permutation(single, KB))(key_list).astype(jnp.int32)
    run_index = jnp.arange(PANELS, dtype=jnp.int32)[:, None]
    return (orders // CAP * KB + run_index * CAP + orders % CAP).reshape(-1).astype(jnp.int32)


def set_ends(drawn, rng, low, top_value):
    place = [jax.random.randint(jax.random.fold_in(rng, axis), (), 0, length) for axis, length in enumerate(drawn.shape)]
    longest = drawn.shape.index(max(drawn.shape))
    beside = place[:longest] + [(place[longest] + 1) % drawn.shape[longest]] + place[longest + 1:]
    return drawn.at[tuple(place)].set(low).at[tuple(beside)].set(top_value)


def block_scale(rng, dims, cuts, least, top_value):
    def one(axis_at, shards_of):
        steps = jax.random.uniform(jax.random.fold_in(jax.random.fold_in(rng, 6), axis_at), (shards_of,), jnp.float32, least / len(cuts), top_value / len(cuts))
        return jnp.repeat(jnp.exp(steps), dims[axis_at] // shards_of).reshape((-1,) + (1,) * (len(dims) - axis_at - 1))

    level = one(*cuts[0])
    for cut in cuts[1:]:
        level = level * one(*cut)
    return level


def centred(own_key, dims, deviation, bound, pieces=(), kind=jnp.bfloat16):
    factor_of = block_scale(own_key, dims, pieces, -0.22, 0.18) if pieces else 1.0
    array = jax.random.normal(own_key, dims, jnp.float32) * deviation * factor_of
    return jnp.minimum(jnp.maximum(array, -bound), bound).astype(kind)


def setup_inputs(seed: int = 0) -> dict:
    streams_of = jax.random.split(jax.random.key(seed), 7)
    return {
        "at": centred(streams_of[0], (PANELS * KB * BS, PANELS * RB * BS), (2 * KB * BS) ** -0.5, 0.09375, ((0, 16), (1, 8))),
        "bmat": centred(streams_of[1], (PANELS * KB * BS, PANELS * CB * BS), 1.0, 6.0, ((0, 8), (1, 16))),
        "mask_a": set_ends((jax.random.randint(streams_of[2], (PANELS * KB, PANELS * RB), 0, 4) < 3).astype(jnp.int32), jax.random.fold_in(streams_of[2], 1), 0, 1),
        "mask_b": set_ends((jax.random.randint(streams_of[3], (PANELS * KB, PANELS * CB), 0, 4) < 3).astype(jnp.int32), jax.random.fold_in(streams_of[3], 1), 0, 1),
        "filt": set_ends((jax.random.randint(streams_of[4], (PANELS * RB, PANELS * CB), 0, 4) < 3).astype(jnp.int32), jax.random.fold_in(streams_of[4], 1), 0, 1),
        "kdist": draw_kdist(jax.random.fold_in(streams_of[6], 71), 0),
    }


def expand(mask):
    widened = jnp.repeat(mask.astype(jnp.bfloat16), BS, axis=0)
    return jnp.repeat(widened, BS, axis=1)


def reference(at, bmat, mask_a, mask_b, filt, kdist):
    a_masked = (at * expand(mask_a)).reshape(PANELS * KB, BS, PANELS * RB * BS)
    b_masked = (bmat * expand(mask_b)).reshape(PANELS * KB, BS, PANELS * CB * BS)
    a_perm = jnp.zeros_like(a_masked).at[kdist].set(a_masked).reshape(PANELS, KB * BS, PANELS, RB * BS)
    b_perm = jnp.zeros_like(b_masked).at[kdist].set(b_masked).reshape(PANELS, KB * BS, PANELS, CB * BS)
    columns = jnp.arange(PANELS, dtype=jnp.int32)

    def one_group(group_id):
        a_rows = lax.dynamic_index_in_dim(a_perm, group_id, axis=2, keepdims=False)
        summed = jnp.zeros((PANELS, RB * BS, CB * BS), jnp.float32)
        for stop_id in range(2):
            chosen = (group_id + columns + stop_id) % PANELS
            a_sel = a_rows[chosen].astype(jnp.float32)
            b_sel = b_perm[chosen, :, columns, :].astype(jnp.float32)
            summed = summed + jnp.einsum("rka,rkb->rab", a_sel, b_sel, precision=lax.Precision.HIGHEST)
        return summed

    blocks = lax.map(one_group, columns)
    whole = blocks.transpose(0, 2, 1, 3).reshape(PANELS * RB * BS, PANELS * CB * BS)
    return whole * expand(filt).astype(jnp.float32)
```

```python
import jax
import jax.numpy as jnp
from jax import lax
from jax.experimental import pallas as pl
from jax.experimental.pallas import tpu as pltpu
from jax.sharding import PartitionSpec as P

BS = 64
KB = 32
NP = 16
W = 1024
MIB = 1 << 20
Y_GROUPS = [list(range(8)), list(range(8, 16))]


def spread(mask, width):
    count = mask.shape[1]
    lane = lax.broadcasted_iota(jnp.int32, (count, width), 1) // BS
    entry = lax.broadcasted_iota(jnp.int32, (count, width), 0)
    chosen = jnp.where(lane == entry, 1.0, 0.0).astype(jnp.bfloat16)
    return jnp.dot(
        mask.astype(jnp.float32).astype(jnp.bfloat16), chosen, preferred_element_type=jnp.float32
    )


def prep_a(ids, kdist, mask, at, to_y, to_z, to_odd, wide, held, sems):
    step = pl.program_id(0)
    row_id, col_id = ids[0], ids[1]
    half = row_id // 8

    @pl.when(step == 0)
    def _():
        wide[...] = spread(mask[...], 2 * W)

    for b in range(4):
        block = step * 4 + b
        gain = wide[pl.ds(block, 1), :].astype(jnp.bfloat16)
        rows = pl.ds(pl.multiple_of(block * BS, BS), BS)
        held[rows, :] = at[b * BS:(b + 1) * BS, :] * gain
        pos = kdist[row_id * KB + block]
        inner = pl.ds(pl.multiple_of((pos % KB - 2 * row_id) * BS, BS), BS)
        for t in range(2):
            tile = (pos // KB - 2 * col_id - t + 2 * NP) % NP
            cols = pl.ds(t * W, W)
            src = held.at[rows, cols]
            near = (tile - 8 * half + NP) % NP
            far = (near + 8) % NP
            even = tile % 2 == 0

            @pl.when(even & (near < 8))
            def _():
                pltpu.make_async_copy(src, to_y.at[near, inner, cols], sems.at[0]).start()

            @pl.when(even & (near > 0) & (near <= 8))
            def _():
                pltpu.make_async_copy(src, to_y.at[near - 1, inner, cols], sems.at[0]).start()

            @pl.when(even & (far <= 8))
            def _():
                pltpu.make_async_copy(src, to_z.at[far // 2, inner, cols], sems.at[1]).start()

            @pl.when(tile % 2 == 1)
            def _():
                pltpu.make_async_copy(src, to_odd.at[tile - 1 + t, inner, :], sems.at[2]).start()

    @pl.when(step == pl.num_programs(0) - 1)
    def _():
        for n, ref in enumerate((to_y, to_z, to_odd)):
            pltpu.make_async_copy(ref, ref, sems.at[n]).wait()


def prep_b(ids, kdist, mask, bmat, x0, x1, x2, x3, to_z, wide, held, sems):
    step = pl.program_id(0)
    row_id, col_id = ids[0], ids[1]
    half, here = col_id // 4, col_id % 4
    to_x = (x0, x1, x2, x3)

    @pl.when(step == 0)
    def _():
        wide[...] = spread(mask[...], W)

    for b in range(8):
        block = step * 8 + b
        gain = wide[pl.ds(block, 1), :].astype(jnp.bfloat16)
        rows = pl.ds(pl.multiple_of(block * BS, BS), BS)
        held[rows, :] = bmat[b * BS:(b + 1) * BS, :] * gain
        pos = kdist[col_id * 2 * KB + block]
        inner = pl.ds(pl.multiple_of((pos % KB - 4 * col_id) * BS, BS), BS)
        tile = (pos // KB - row_id + NP) % NP
        src = held.at[rows, :]
        near = (tile - 8 * half + NP) % NP
        far = (near + 8) % NP
        even = tile % 2 == 0
        first = (near // 2 - here + 4) % 4
        second = (near // 2 - 1 - here + 8) % 4
        odd_at = (tile // 2 - here + 8) % 4
        odd_kind = jnp.where(tile // 8 == half, 1, 3)
        for hop in range(4):

            @pl.when(even & (near < 8) & (first == hop))
            def _():
                pltpu.make_async_copy(src, to_x[hop].at[0, inner, :], sems.at[hop]).start()

            @pl.when(even & (near > 0) & (near <= 8) & (second == hop))
            def _():
                pltpu.make_async_copy(src, to_x[hop].at[2, inner, :], sems.at[hop]).start()

            @pl.when((tile % 2 == 1) & (odd_at == hop))
            def _():
                pltpu.make_async_copy(src, to_x[hop].at[odd_kind, inner, :], sems.at[hop]).start()

        @pl.when(even & (far <= 8))
        def _():
            pltpu.make_async_copy(src, to_z.at[far // 2, inner, :], sems.at[4]).start()

    @pl.when(step == pl.num_programs(0) - 1)
    def _():
        for n, ref in enumerate((x0, x1, x2, x3, to_z)):
            pltpu.make_async_copy(ref, ref, sems.at[n]).wait()


def multiply(ids, filt, e_near, e_far, o_mine, o_swap, r0, r1, r2, r3, p0, p1, p2, p3, q,
             out, e_v, o_v, b_v, wide, sems):
    row_id, col_id = ids[0], ids[1]
    core = row_id % 2
    a_half = row_id // 8
    b_half, here = col_id // 4, col_id % 4
    copies = []

    def fetch(src, dst):
        copy = pltpu.make_async_copy(src, dst, sems.at[len(copies)])
        copy.start()
        copies.append(copy)

    def half_rows(which):
        return pl.ds(pl.multiple_of(which * W, W), W)

    fetch(e_near, e_v.at[half_rows(a_half)])
    fetch(e_far, e_v.at[half_rows(1 - a_half)])
    fetch(o_mine, o_v.at[core])
    fetch(o_swap, o_v.at[1 - core])
    for hop, (near, far) in enumerate(zip((r0, r1, r2, r3), (p0, p1, p2, p3))):
        place = (here - hop + 4) % 4
        mine = pl.ds(pl.multiple_of((b_half * 4 + place) * 256, 256), 256)
        other = pl.ds(pl.multiple_of(((1 - b_half) * 4 + place) * 256, 256), 256)
        fetch(near.at[pl.ds(0, 3)], b_v.at[:, mine])
        fetch(far.at[0], b_v.at[0, other])
        fetch(far.at[1], b_v.at[2, other])
        fetch(q.at[hop], b_v.at[1, other])
    wide[...] = spread(filt[...], W)
    for copy in copies:
        copy.wait()
    contract = (((0,), (0,)), ((), ()))
    for t in range(2):
        for m in range(4):
            col = t * W + m * 256
            left = e_v[:, col:col + 256]
            total = lax.dot_general(left, b_v[t + core], contract, preferred_element_type=jnp.float32)
            left = o_v[t, :, m * 256:(m + 1) * 256]
            total += lax.dot_general(left, b_v[t + 1 - core], contract, preferred_element_type=jnp.float32)
            for i in range(4):
                block = col // BS + i
                gain = wide[block:block + 1, :]
                out[block * BS:(block + 1) * BS, :] = total[i * BS:(i + 1) * BS, :] * gain


SMEM = pl.BlockSpec(memory_space=pltpu.SMEM)
ANY = pl.BlockSpec(memory_space=pl.ANY)
VMEM = pl.BlockSpec(memory_space=pltpu.VMEM)


def bf16(*shape):
    return jax.ShapeDtypeStruct(shape, jnp.bfloat16)


def on_device(at, bmat, mask_a, mask_b, filt, kdist):
    row_id = lax.axis_index("row")
    col_id = lax.axis_index("col")
    ids = jnp.stack([row_id, col_id]).astype(jnp.int32)
    here = col_id % 4

    def swap_z_hi(value):
        return lax.ppermute(value, "row", [(i, i ^ 8) for i in range(16)])

    def swap_z_lo(value):
        return lax.ppermute(value, "col", [(i, i ^ 4) for i in range(8)])

    def along_x(value, hop):
        return lax.ppermute(value, "col", [(i, i // 4 * 4 + (i % 4 + hop) % 4) for i in range(8)])

    x0, x1, x2, x3, b_z = pl.pallas_call(
        prep_b,
        grid=(8,),
        out_shape=[bf16(4, 256, W)] * 4 + [bf16(5, 256, W)],
        in_specs=[SMEM, SMEM, pl.BlockSpec((64, 16), lambda s: (0, 0)),
                  pl.BlockSpec((512, W), lambda s: (s, 0))],
        out_specs=[ANY] * 5,
        scratch_shapes=[pltpu.VMEM((64, W), jnp.float32), pltpu.VMEM((4096, W), jnp.bfloat16),
                        pltpu.SemaphoreType.DMA((5,))],
        compiler_params=pltpu.CompilerParams(vmem_limit_bytes=32 * MIB),
        name="prep_b",
    )(ids, kdist, mask_b, bmat)
    a_y, a_z, a_odd = pl.pallas_call(
        prep_a,
        grid=(8,),
        out_shape=[bf16(8, 128, 2 * W), bf16(5, 128, 2 * W), bf16(16, 128, W)],
        in_specs=[SMEM, SMEM, pl.BlockSpec((32, 32), lambda s: (0, 0)),
                  pl.BlockSpec((256, 2 * W), lambda s: (s, 0))],
        out_specs=[ANY] * 3,
        scratch_shapes=[pltpu.VMEM((32, 2 * W), jnp.float32), pltpu.VMEM((2048, 2 * W), jnp.bfloat16),
                        pltpu.SemaphoreType.DMA((3,))],
        compiler_params=pltpu.CompilerParams(vmem_limit_bytes=32 * MIB),
        name="prep_a",
    )(ids, kdist, mask_a, at)

    a_cross = swap_z_hi(a_z)
    b_cross = swap_z_lo(b_z)
    e_near = lax.all_to_all(a_y, "row", 0, 0, axis_index_groups=Y_GROUPS, tiled=True)
    r1, r2, r3 = along_x(x1, 1), along_x(x2, 2), along_x(x3, 3)
    o_mine = lax.all_to_all(a_odd, "row", 0, 0, tiled=True)
    o_swap = lax.ppermute(o_mine, "row", [(i, i ^ 1) for i in range(16)])

    q_send = jnp.concatenate([v[3:4] for v in (x0, r1, r2, r3)], axis=0)
    q_send, a_cross, b_cross = lax.optimization_barrier((q_send, a_cross, b_cross))
    q = swap_z_lo(q_send)
    far = [lax.dynamic_slice_in_dim(b_cross, (here + hop) % 4, 2, 0) for hop in range(4)]
    p1, p2, p3 = along_x(far[1], 1), along_x(far[2], 2), along_x(far[3], 3)
    a_again = jnp.stack([a_cross[:4], a_cross[1:]], axis=1).reshape(8, 128, 2 * W)
    e_far = lax.all_to_all(a_again, "row", 0, 0, axis_index_groups=Y_GROUPS, tiled=True)

    return pl.pallas_call(
        multiply,
        out_shape=jax.ShapeDtypeStruct((2 * W, W), jnp.float32),
        in_specs=[SMEM, VMEM] + [ANY] * 13,
        out_specs=VMEM,
        scratch_shapes=[pltpu.VMEM((2048, 2 * W), jnp.bfloat16), pltpu.VMEM((2, 2048, W), jnp.bfloat16),
                        pltpu.VMEM((3, 2048, W), jnp.bfloat16), pltpu.VMEM((32, W), jnp.float32),
                        pltpu.SemaphoreType.DMA((20,))],
        compiler_params=pltpu.CompilerParams(vmem_limit_bytes=56 * MIB),
        name="multiply",
    )(ids, filt, e_near.reshape(W, 2 * W), e_far.reshape(W, 2 * W), o_mine.reshape(2 * W, W),
      o_swap.reshape(2 * W, W), x0, r1, r2, r3, far[0], p1, p2, p3, q)


def solution(mesh):
    in_specs = (
        P("row", "col"),
        P("col", "row"),
        P("row", "col"),
        P("col", "row"),
        P("col", "row"),
        P(),
    )
    out_specs = P("col", "row")
    return jax.shard_map(
        on_device, mesh=mesh, in_specs=in_specs, out_specs=out_specs, check_vma=False
    )
```

```python
import jax
import jax.numpy as jnp
from jax import lax
from jax.experimental import pallas as pl
from jax.experimental.pallas import tpu as pltpu
from jax.sharding import PartitionSpec as P

BS = 64
KB = 32
NP = 16
W = 1024
MIB = 1 << 20
Y_GROUPS = [list(range(8)), list(range(8, 16))]


def spread(mask, width):
    count = mask.shape[1]
    lane = lax.broadcasted_iota(jnp.int32, (count, width), 1) // BS
    entry = lax.broadcasted_iota(jnp.int32, (count, width), 0)
    chosen = jnp.where(lane == entry, 1.0, 0.0).astype(jnp.bfloat16)
    return jnp.dot(
        mask.astype(jnp.float32).astype(jnp.bfloat16), chosen, preferred_element_type=jnp.float32
    )


def prep_a(ids, kdist, mask, at, to_y, to_z, wide, held, in_sems, sems):
    row_id, col_id = ids[0], ids[1]
    half = row_id // 8

    def chunk(n):
        rows = pl.ds(n * 256, 256)
        return pltpu.make_async_copy(at.at[rows], held.at[rows], in_sems.at[n])

    for n in range(8):
        chunk(n).start()
    wide[...] = spread(mask[...], 2 * W)
    for block in range(KB):
        if block % 4 == 0:
            chunk(block // 4).wait()
        gain = wide[block:block + 1, :].astype(jnp.bfloat16)
        rows = pl.ds(block * BS, BS)
        held[rows, :] = held[rows, :] * gain
        pos = kdist[row_id * KB + block]
        slot = (pos % KB - 2 * row_id) * BS
        inner = pl.ds(pl.multiple_of(slot, BS), BS)
        for t in range(2):
            tile = (pos // KB - 2 * col_id - t + 2 * NP) % NP
            cols = pl.ds(t * W, W)
            src = held.at[rows, cols]
            near = (tile - 8 * half + NP) % NP
            far = (near + 8) % NP
            odd = tile % 2 == 1
            even = tile % 2 == 0
            first = jnp.where(odd, tile // 2 % 4 * 2 + t, near)
            first_row = jnp.where(odd, 128, 0) + slot
            first_col = jnp.where(odd, jnp.where(tile // 8 == half, 0, W), t * W)

            @pl.when(odd | (near < 8))
            def _():
                dst = to_y.at[first, pl.ds(pl.multiple_of(first_row, BS), BS), pl.ds(pl.multiple_of(first_col, W), W)]
                pltpu.make_async_copy(src, dst, sems.at[0]).start()

            @pl.when(even & (near > 0) & (near <= 8))
            def _():
                pltpu.make_async_copy(src, to_y.at[near - 1, inner, cols], sems.at[0]).start()

            @pl.when(even & (far <= 8))
            def _():
                pltpu.make_async_copy(src, to_z.at[far // 2, inner, cols], sems.at[1]).start()

    for n, ref in enumerate((to_y, to_z)):
        pltpu.make_async_copy(ref, ref, sems.at[n]).wait()


def prep_b(ids, kdist, mask, bmat, x0, x1, x2, x3, to_z, wide, held, in_sems, sems):
    row_id, col_id = ids[0], ids[1]
    half, here = col_id // 4, col_id % 4
    to_x = (x0, x1, x2, x3)

    def chunk(n):
        rows = pl.ds(n * 512, 512)
        return pltpu.make_async_copy(bmat.at[rows], held.at[rows], in_sems.at[n])

    for n in range(8):
        chunk(n).start()
    wide[...] = spread(mask[...], W)
    for block in range(2 * KB):
        if block % 8 == 0:
            chunk(block // 8).wait()
        gain = wide[block:block + 1, :].astype(jnp.bfloat16)
        rows = pl.ds(block * BS, BS)
        held[rows, :] = held[rows, :] * gain
        pos = kdist[col_id * 2 * KB + block]
        inner = pl.ds(pl.multiple_of((pos % KB - 4 * col_id) * BS, BS), BS)
        tile = (pos // KB - row_id + NP) % NP
        src = held.at[rows, :]
        near = (tile - 8 * half + NP) % NP
        far = (near + 8) % NP
        odd = tile % 2 == 1
        even = tile % 2 == 0
        first = (jnp.where(odd, tile, near) // 2 - here + 8) % 4
        kind = jnp.where(odd, jnp.where(tile // 8 == half, 1, 3), 0)
        second = (near // 2 - 1 - here + 8) % 4

        def send(hop, kind):
            def to(n):
                def run():
                    pltpu.make_async_copy(src, to_x[n].at[kind, inner, :], sems.at[n]).start()

                return run

            lax.cond(hop < 2, lambda: lax.cond(hop == 0, to(0), to(1)), lambda: lax.cond(hop == 2, to(2), to(3)))

        @pl.when(odd | (near < 8))
        def _():
            send(first, kind)

        @pl.when(even & (near > 0) & (near <= 8))
        def _():
            send(second, 2)

        @pl.when(even & (far <= 8))
        def _():
            pltpu.make_async_copy(src, to_z.at[far // 2, inner, :], sems.at[4]).start()

    for n, ref in enumerate((x0, x1, x2, x3, to_z)):
        pltpu.make_async_copy(ref, ref, sems.at[n]).wait()


CONTRACT = (((0,), (0,)), ((), ()))


def product(left, right):
    return lax.dot_general(left, right, CONTRACT, preferred_element_type=jnp.float32)


def multiply(ids, near_a, e_far, o_near, o_cross, o_swap, r0, r1, r2, r3, p0, p1, p2, p3,
             out, left_out, left_v, b_v, sems, out_sem):
    row_id, col_id = ids[0], ids[1]
    core = row_id % 2
    a_half = row_id // 8
    b_half, here = col_id // 4, col_id % 4
    copies = []

    def fetch(src, dst):
        copy = pltpu.make_async_copy(src, dst, sems.at[len(copies)])
        copy.start()
        copies.append(copy)

    def group(which):
        return pl.ds(pl.multiple_of(which * W, W), W)

    sources = pl.ds(0, 8)
    a_near = pl.ds(pl.multiple_of(a_half * 8, 8), 8)
    a_far = pl.ds(pl.multiple_of(8 - a_half * 8, 8), 8)
    fetch(near_a.at[sources, pl.ds(0, 128), group(core)], left_v.at[0, core, a_near])
    fetch(near_a.at[sources, pl.ds(0, 128), group(1 - core)], left_v.at[1, 1 - core, a_near])
    fetch(near_a.at[sources, pl.ds(128, 128), group(0)], left_v.at[1, core, a_near])
    fetch(o_near, left_v.at[0, 1 - core, a_near])
    for hop, near in enumerate((r0, r1, r2, r3)):
        place = (here - hop + 4) % 4
        fetch(near.at[pl.ds(0, 3)], b_v.at[:, pl.ds(pl.multiple_of((b_half * 4 + place) * 256, 256), 256)])
    for hop, far in enumerate((p0, p1, p2, p3)):
        place = (here - hop + 4) % 4
        rows = pl.ds(pl.multiple_of(((1 - b_half) * 4 + place) * 256, 256), 256)
        fetch(far.at[0], b_v.at[0, rows])
        fetch(far.at[1], b_v.at[2, rows])
    fetch(e_far.at[sources, :, group(core)], left_v.at[0, core, a_far])
    fetch(e_far.at[sources, :, group(1 - core)], left_v.at[1, 1 - core, a_far])
    fetch(o_cross, left_v.at[1, core, a_far])
    fetch(o_swap, left_v.at[0, 1 - core, a_far])
    for copy in copies:
        copy.wait()
    later = []
    for t in range(2):
        for hop in range(4):
            place = (here - hop + 4) % 4
            part = pltpu.make_async_copy(
                left_v.at[1, t, pl.ds((1 - b_half) * 8 + place * 2, 2)],
                left_out.at[t, pl.ds(hop * 2, 2)], out_sem.at[t * 4 + hop])
            part.start()
            later.append(part)
    near_rows = pl.ds(pl.multiple_of(b_half * W, W), W)
    near_pieces = pl.ds(pl.multiple_of(b_half * 8, 8), 8)
    for t in range(2):
        for m in range(4):
            cols = slice(m * 256, (m + 1) * 256)
            total = product(left_v[0, t, :, :, cols].reshape(2 * W, 256), b_v[2 * t])
            total += product(left_v[1, t, near_pieces, :, cols].reshape(W, 256), b_v[1, near_rows])
            out[t * W + m * 256:t * W + (m + 1) * 256, :] = total
    for part in later:
        part.wait()


def finish(filt, part, left, right, out, wide):
    step = pl.program_id(0)

    @pl.when(step == 0)
    def _():
        wide[...] = spread(filt[...], W)

    total = part[...] + product(left[...].reshape(W, 256), right[...].reshape(W, W))
    for i in range(4):
        rows = slice(i * BS, (i + 1) * BS)
        out[rows, :] = total[rows, :] * wide[pl.ds(step * 4 + i, 1), :]


SMEM = pl.BlockSpec(memory_space=pltpu.SMEM)
ANY = pl.BlockSpec(memory_space=pl.ANY)
HBM = pl.BlockSpec(memory_space=pltpu.HBM)
VMEM = pl.BlockSpec(memory_space=pltpu.VMEM)


def bf16(*shape):
    return jax.ShapeDtypeStruct(shape, jnp.bfloat16)


def on_device(at, bmat, mask_a, mask_b, filt, kdist):
    row_id = lax.axis_index("row")
    col_id = lax.axis_index("col")
    ids = jnp.stack([row_id, col_id]).astype(jnp.int32)
    here = col_id % 4

    def swap_z_hi(value):
        return lax.ppermute(value, "row", [(i, i ^ 8) for i in range(16)])

    def swap_z_lo(value):
        return lax.ppermute(value, "col", [(i, i ^ 4) for i in range(8)])

    def swap_core(value):
        return lax.ppermute(value, "row", [(i, i ^ 1) for i in range(16)])

    def along_x(value, hop):
        return lax.ppermute(value, "col", [(i, i // 4 * 4 + (i % 4 + hop) % 4) for i in range(8)])

    def along_y(value):
        return lax.all_to_all(value, "row", 0, 0, axis_index_groups=Y_GROUPS, tiled=True)

    a_y, a_z = pl.pallas_call(
        prep_a,
        out_shape=[bf16(8, 256, 2 * W), bf16(5, 128, 2 * W)],
        in_specs=[SMEM, SMEM, VMEM, HBM],
        out_specs=[ANY] * 2,
        scratch_shapes=[pltpu.VMEM((32, 2 * W), jnp.float32), pltpu.VMEM((2048, 2 * W), jnp.bfloat16),
                        pltpu.SemaphoreType.DMA((8,)), pltpu.SemaphoreType.DMA((2,))],
        compiler_params=pltpu.CompilerParams(vmem_limit_bytes=24 * MIB),
        name="prep_a",
    )(ids, kdist, mask_a, pltpu.with_memory_space_constraint(at, pltpu.HBM))
    x0, x1, x2, x3, b_z = pl.pallas_call(
        prep_b,
        out_shape=[bf16(4, 256, W)] * 4 + [bf16(5, 256, W)],
        in_specs=[SMEM, SMEM, VMEM, HBM],
        out_specs=[ANY] * 5,
        scratch_shapes=[pltpu.VMEM((64, W), jnp.float32), pltpu.VMEM((4096, W), jnp.bfloat16),
                        pltpu.SemaphoreType.DMA((8,)), pltpu.SemaphoreType.DMA((5,))],
        compiler_params=pltpu.CompilerParams(vmem_limit_bytes=24 * MIB),
        name="prep_b",
    )(ids, kdist, mask_b, pltpu.with_memory_space_constraint(bmat, pltpu.HBM))

    a_cross = swap_z_hi(a_z)
    b_cross = swap_z_lo(b_z)
    near_a = along_y(a_y)
    r1, r2, r3 = along_x(x1, 1), along_x(x2, 2), along_x(x3, 3)

    o_cross = swap_z_hi(near_a[:, 128:, W:])
    o_near = swap_core(near_a[:, 128:, :W])

    q_send = jnp.concatenate([v[3:4] for v in (x0, r1, r2, r3)], axis=0)
    q_send, a_cross, b_cross = lax.optimization_barrier((q_send, a_cross, b_cross))
    q = swap_z_lo(q_send)
    far = [lax.dynamic_slice_in_dim(b_cross, (here + hop) % 4, 2, 0) for hop in range(4)]
    p1, p2, p3 = along_x(far[1], 1), along_x(far[2], 2), along_x(far[3], 3)
    e_far = along_y(jnp.stack([a_cross[:4], a_cross[1:]], axis=1).reshape(8, 128, 2 * W))

    o_cross, p1, p2, p3 = lax.optimization_barrier((o_cross, p1, p2, p3))
    o_swap = swap_core(o_cross)

    part, left = pl.pallas_call(
        multiply,
        out_shape=[jax.ShapeDtypeStruct((2 * W, W), jnp.float32), bf16(2, 8, 128, W)],
        in_specs=[SMEM] + [ANY] * 13,
        out_specs=[VMEM, ANY],
        scratch_shapes=[pltpu.VMEM((2, 2, 16, 128, W), jnp.bfloat16), pltpu.VMEM((3, 2048, W), jnp.bfloat16),
                        pltpu.SemaphoreType.DMA((20,)), pltpu.SemaphoreType.DMA((8,))],
        compiler_params=pltpu.CompilerParams(vmem_limit_bytes=52 * MIB),
        name="multiply",
    )(ids, near_a, e_far, o_near, o_cross, o_swap, x0, r1, r2, r3, far[0], p1, p2, p3)
    return pl.pallas_call(
        finish,
        grid=(8,),
        out_shape=jax.ShapeDtypeStruct((2 * W, W), jnp.float32),
        in_specs=[pl.BlockSpec((32, 16), lambda s: (0, 0)), pl.BlockSpec((256, W), lambda s: (s, 0)),
                  pl.BlockSpec((None, 8, 128, 256), lambda s: (s // 4, 0, 0, s % 4)),
                  pl.BlockSpec((4, 256, W), lambda s: (0, 0, 0))],
        out_specs=pl.BlockSpec((256, W), lambda s: (s, 0)),
        scratch_shapes=[pltpu.VMEM((32, W), jnp.float32)],
        compiler_params=pltpu.CompilerParams(vmem_limit_bytes=32 * MIB),
        name="finish",
    )(filt, part, left, q)


def solution(mesh):
    in_specs = (
        P("row", "col"),
        P("col", "row"),
        P("row", "col"),
        P("col", "row"),
        P("col", "row"),
        P(),
    )
    out_specs = P("col", "row")
    return jax.shard_map(
        on_device, mesh=mesh, in_specs=in_specs, out_specs=out_specs, check_vma=False
    )
```

```python
import jax
import jax.numpy as jnp
from jax import lax
from jax.experimental import pallas as pl
from jax.experimental.pallas import tpu as pltpu
from jax.sharding import PartitionSpec as P

BS = 64
KB = 32
NP = 16
W = 1024
MIB = 1 << 20
Y_GROUPS = [list(range(8)), list(range(8, 16))]


def spread(mask, width):
    count = mask.shape[1]
    lane = lax.broadcasted_iota(jnp.int32, (count, width), 1) // BS
    entry = lax.broadcasted_iota(jnp.int32, (count, width), 0)
    chosen = jnp.where(lane == entry, 1.0, 0.0).astype(jnp.bfloat16)
    return jnp.dot(
        mask.astype(jnp.float32).astype(jnp.bfloat16), chosen, preferred_element_type=jnp.float32
    )


def prep_a(ids, kdist, mask, at, to_y, to_z, wide, held, in_sems, sems):
    row_id, col_id = ids[0], ids[1]
    half = row_id // 8

    def chunk(n):
        rows = pl.ds(n * 256, 256)
        return pltpu.make_async_copy(at.at[rows], held.at[rows], in_sems.at[n])

    for n in range(8):
        chunk(n).start()
    wide[...] = spread(mask[...], 2 * W)
    for block in range(KB):
        if block % 4 == 0:
            chunk(block // 4).wait()
        gain = wide[block:block + 1, :].astype(jnp.bfloat16)
        rows = pl.ds(block * BS, BS)
        held[rows, :] = held[rows, :] * gain
        pos = kdist[row_id * KB + block]
        slot = (pos % KB - 2 * row_id) * BS
        inner = pl.ds(pl.multiple_of(slot, BS), BS)
        for t in range(2):
            tile = (pos // KB - 2 * col_id - t + 2 * NP) % NP
            cols = pl.ds(t * W, W)
            src = held.at[rows, cols]
            near = (tile - 8 * half + NP) % NP
            far = (near + 8) % NP
            odd = tile % 2 == 1
            even = tile % 2 == 0
            first = jnp.where(odd, tile // 2 % 4 * 2 + t, near)
            first_row = jnp.where(odd, jnp.where(tile // 8 == half, 256, 384), t * 128) + slot

            @pl.when(odd | (near < 8))
            def _():
                dst = to_y.at[first, pl.ds(pl.multiple_of(first_row, BS), BS), :]
                pltpu.make_async_copy(src, dst, sems.at[0]).start()

            @pl.when(even & (near > 0) & (near <= 8))
            def _():
                pltpu.make_async_copy(src, to_y.at[near - 1, pl.ds(pl.multiple_of(t * 128 + slot, BS), BS), :], sems.at[0]).start()

            @pl.when(even & (far <= 8))
            def _():
                pltpu.make_async_copy(src, to_z.at[far // 2, inner, cols], sems.at[1]).start()

    for n, ref in enumerate((to_y, to_z)):
        pltpu.make_async_copy(ref, ref, sems.at[n]).wait()


def prep_b(ids, kdist, mask, bmat, x0, x1, x2, x3, to_z, wide, held, in_sems, sems):
    row_id, col_id = ids[0], ids[1]
    half, here = col_id // 4, col_id % 4
    to_x = (x0, x1, x2, x3)

    def chunk(n):
        rows = pl.ds(n * 512, 512)
        return pltpu.make_async_copy(bmat.at[rows], held.at[rows], in_sems.at[n])

    for n in range(8):
        chunk(n).start()
    wide[...] = spread(mask[...], W)
    for block in range(2 * KB):
        if block % 8 == 0:
            chunk(block // 8).wait()
        gain = wide[block:block + 1, :].astype(jnp.bfloat16)
        rows = pl.ds(block * BS, BS)
        held[rows, :] = held[rows, :] * gain
        pos = kdist[col_id * 2 * KB + block]
        inner = pl.ds(pl.multiple_of((pos % KB - 4 * col_id) * BS, BS), BS)
        tile = (pos // KB - row_id + NP) % NP
        src = held.at[rows, :]
        near = (tile - 8 * half + NP) % NP
        far = (near + 8) % NP
        odd = tile % 2 == 1
        even = tile % 2 == 0
        first = (jnp.where(odd, tile, near) // 2 - here + 8) % 4
        kind = jnp.where(odd, jnp.where(tile // 8 == half, 1, 3), 0)
        second = (near // 2 - 1 - here + 8) % 4

        def send(hop, kind):
            def to(n):
                def run():
                    pltpu.make_async_copy(src, to_x[n].at[kind, inner, :], sems.at[n]).start()

                return run

            lax.cond(hop < 2, lambda: lax.cond(hop == 0, to(0), to(1)), lambda: lax.cond(hop == 2, to(2), to(3)))

        @pl.when(odd | (near < 8))
        def _():
            send(first, kind)

        @pl.when(even & (near > 0) & (near <= 8))
        def _():
            send(second, 2)

        @pl.when(even & (far <= 8))
        def _():
            pltpu.make_async_copy(src, to_z.at[far // 2, inner, :], sems.at[4]).start()

    for n, ref in enumerate((x0, x1, x2, x3, to_z)):
        pltpu.make_async_copy(ref, ref, sems.at[n]).wait()


CONTRACT = (((0,), (0,)), ((), ()))


def product(left, right):
    return lax.dot_general(left, right, CONTRACT, preferred_element_type=jnp.float32)


def multiply(ids, near_a, e_far, o_near, o_cross, o_swap, r0, r1, r2, r3, p0, p1, p2, p3,
             out, left_out, left_v, b_v, sems, out_sem):
    row_id, col_id = ids[0], ids[1]
    core = row_id % 2
    a_half = row_id // 8
    b_half, here = col_id // 4, col_id % 4
    copies = []

    def fetch(src, dst):
        copy = pltpu.make_async_copy(src, dst, sems.at[len(copies)])
        copy.start()
        copies.append(copy)

    def group(which):
        return pl.ds(pl.multiple_of(which * W, W), W)

    sources = pl.ds(0, 8)
    a_near = pl.ds(pl.multiple_of(a_half * 8, 8), 8)
    a_far = pl.ds(pl.multiple_of(8 - a_half * 8, 8), 8)
    fetch(near_a.at[sources, pl.ds(pl.multiple_of(core * 128, 128), 128)], left_v.at[0, core, a_near])
    fetch(near_a.at[sources, pl.ds(pl.multiple_of(128 - core * 128, 128), 128)], left_v.at[1, 1 - core, a_near])
    fetch(near_a.at[sources, pl.ds(256, 128)], left_v.at[1, core, a_near])
    fetch(o_near, left_v.at[0, 1 - core, a_near])
    for hop, near in enumerate((r0, r1, r2, r3)):
        place = (here - hop + 4) % 4
        fetch(near.at[pl.ds(0, 3)], b_v.at[:, pl.ds(pl.multiple_of((b_half * 4 + place) * 256, 256), 256)])
    for hop, far in enumerate((p0, p1, p2, p3)):
        place = (here - hop + 4) % 4
        rows = pl.ds(pl.multiple_of(((1 - b_half) * 4 + place) * 256, 256), 256)
        fetch(far.at[0], b_v.at[0, rows])
        fetch(far.at[1], b_v.at[2, rows])
    fetch(e_far.at[sources, :, group(core)], left_v.at[0, core, a_far])
    fetch(e_far.at[sources, :, group(1 - core)], left_v.at[1, 1 - core, a_far])
    fetch(o_cross, left_v.at[1, core, a_far])
    fetch(o_swap, left_v.at[0, 1 - core, a_far])
    for copy in copies:
        copy.wait()
    later = []
    for t in range(2):
        for hop in range(4):
            place = (here - hop + 4) % 4
            part = pltpu.make_async_copy(
                left_v.at[1, t, pl.ds((1 - b_half) * 8 + place * 2, 2)],
                left_out.at[t, pl.ds(hop * 2, 2)], out_sem.at[t * 4 + hop])
            part.start()
            later.append(part)
    near_rows = pl.ds(pl.multiple_of(b_half * W, W), W)
    near_pieces = pl.ds(pl.multiple_of(b_half * 8, 8), 8)
    for t in range(2):
        for m in range(4):
            cols = slice(m * 256, (m + 1) * 256)
            total = product(left_v[0, t, :, :, cols].reshape(2 * W, 256), b_v[2 * t])
            total += product(left_v[1, t, near_pieces, :, cols].reshape(W, 256), b_v[1, near_rows])
            out[t * W + m * 256:t * W + (m + 1) * 256, :] = total
    for part in later:
        part.wait()


def finish(filt, part, left, right, out, wide):
    step = pl.program_id(0)

    @pl.when(step == 0)
    def _():
        wide[...] = spread(filt[...], W)

    total = part[...] + product(left[...].reshape(W, 256), right[...].reshape(W, W))
    for i in range(4):
        rows = slice(i * BS, (i + 1) * BS)
        out[rows, :] = total[rows, :] * wide[pl.ds(step * 4 + i, 1), :]


SMEM = pl.BlockSpec(memory_space=pltpu.SMEM)
ANY = pl.BlockSpec(memory_space=pl.ANY)
HBM = pl.BlockSpec(memory_space=pltpu.HBM)
VMEM = pl.BlockSpec(memory_space=pltpu.VMEM)


def bf16(*shape):
    return pltpu.HBM(shape, jnp.bfloat16)


def in_hbm(*values):
    return [pltpu.with_memory_space_constraint(value, pltpu.HBM) for value in values]


def on_device(at, bmat, mask_a, mask_b, filt, kdist):
    row_id = lax.axis_index("row")
    col_id = lax.axis_index("col")
    ids = jnp.stack([row_id, col_id]).astype(jnp.int32)
    here = col_id % 4

    def swap_z_hi(value):
        return lax.ppermute(value, "row", [(i, i ^ 8) for i in range(16)])

    def swap_z_lo(value):
        return lax.ppermute(value, "col", [(i, i ^ 4) for i in range(8)])

    def swap_core(value):
        return lax.ppermute(value, "row", [(i, i ^ 1) for i in range(16)])

    def along_x(value, hop):
        return lax.ppermute(value, "col", [(i, i // 4 * 4 + (i % 4 + hop) % 4) for i in range(8)])

    def along_y(value):
        return lax.all_to_all(value, "row", 0, 0, axis_index_groups=Y_GROUPS, tiled=True)

    a_y, a_z = pl.pallas_call(
        prep_a,
        out_shape=[bf16(8, 512, W), bf16(5, 128, 2 * W)],
        in_specs=[SMEM, SMEM, VMEM, HBM],
        out_specs=[HBM] * 2,
        scratch_shapes=[pltpu.VMEM((32, 2 * W), jnp.float32), pltpu.VMEM((2048, 2 * W), jnp.bfloat16),
                        pltpu.SemaphoreType.DMA((8,)), pltpu.SemaphoreType.DMA((2,))],
        compiler_params=pltpu.CompilerParams(vmem_limit_bytes=24 * MIB),
        name="prep_a",
    )(ids, kdist, mask_a, pltpu.with_memory_space_constraint(at, pltpu.HBM))
    x0, x1, x2, x3, b_z = pl.pallas_call(
        prep_b,
        out_shape=[bf16(4, 256, W)] * 4 + [bf16(5, 256, W)],
        in_specs=[SMEM, SMEM, VMEM, HBM],
        out_specs=[HBM] * 5,
        scratch_shapes=[pltpu.VMEM((64, W), jnp.float32), pltpu.VMEM((4096, W), jnp.bfloat16),
                        pltpu.SemaphoreType.DMA((8,)), pltpu.SemaphoreType.DMA((5,))],
        compiler_params=pltpu.CompilerParams(vmem_limit_bytes=24 * MIB),
        name="prep_b",
    )(ids, kdist, mask_b, pltpu.with_memory_space_constraint(bmat, pltpu.HBM))

    a_y, a_z, x0, x1, x2, x3, b_z = lax.optimization_barrier((a_y, a_z, x0, x1, x2, x3, b_z))
    a_cross = swap_z_hi(a_z)
    b_cross = swap_z_lo(b_z)
    near_a = along_y(a_y)
    r1, r3 = along_x(x1, 1), along_x(x3, 3)
    x2, r1, r3 = lax.optimization_barrier((x2, r1, r3))
    r2 = along_x(x2, 2)

    o_send = near_a[:, 384:]
    q_send = jnp.concatenate([v[3:4] for v in (x0, r1, r2, r3)], axis=0)
    a_cross, b_cross, near_a, o_send, q_send = lax.optimization_barrier((a_cross, b_cross, near_a, o_send, q_send))
    o_cross = swap_z_hi(o_send)
    o_near = swap_core(near_a[:, 256:384])

    e_far = along_y(jnp.stack([a_cross[:4], a_cross[1:]], axis=1).reshape(8, 128, 2 * W))
    far = [lax.dynamic_slice_in_dim(b_cross, (here + hop) % 4, 2, 0) for hop in range(4)]
    p1, p3 = along_x(far[1], 1), along_x(far[3], 3)
    p2_send, p1, p3 = lax.optimization_barrier((far[2], p1, p3))
    p2 = along_x(p2_send, 2)

    q_send, o_cross, p1, p3 = lax.optimization_barrier((q_send, o_cross, p1, p3))
    q = swap_z_lo(q_send)
    o_swap = swap_core(o_cross)

    part, left = pl.pallas_call(
        multiply,
        out_shape=[jax.ShapeDtypeStruct((2 * W, W), jnp.float32), bf16(2, 8, 128, W)],
        in_specs=[SMEM] + [ANY] * 13,
        out_specs=[VMEM, HBM],
        scratch_shapes=[pltpu.VMEM((2, 2, 16, 128, W), jnp.bfloat16), pltpu.VMEM((3, 2048, W), jnp.bfloat16),
                        pltpu.SemaphoreType.DMA((20,)), pltpu.SemaphoreType.DMA((8,))],
        compiler_params=pltpu.CompilerParams(vmem_limit_bytes=52 * MIB),
        name="multiply",
    )(ids, near_a, e_far, o_near, o_cross, o_swap, x0, r1, r2, r3, far[0], p1, p2, p3)
    return pl.pallas_call(
        finish,
        grid=(8,),
        out_shape=jax.ShapeDtypeStruct((2 * W, W), jnp.float32),
        in_specs=[pl.BlockSpec((32, 16), lambda s: (0, 0)), pl.BlockSpec((256, W), lambda s: (s, 0)),
                  pl.BlockSpec((None, 8, 128, 256), lambda s: (s // 4, 0, 0, s % 4)),
                  pl.BlockSpec((4, 256, W), lambda s: (0, 0, 0))],
        out_specs=pl.BlockSpec((256, W), lambda s: (s, 0)),
        scratch_shapes=[pltpu.VMEM((32, W), jnp.float32)],
        compiler_params=pltpu.CompilerParams(vmem_limit_bytes=32 * MIB),
        name="finish",
    )(filt, *in_hbm(part, left), q)


def solution(mesh):
    in_specs = (
        P("row", "col"),
        P("col", "row"),
        P("row", "col"),
        P("col", "row"),
        P("col", "row"),
        P(),
    )
    out_specs = P("col", "row")
    return jax.shard_map(
        on_device, mesh=mesh, in_specs=in_specs, out_specs=out_specs, check_vma=False
    )
```

```python
import jax
import jax.numpy as jnp
from jax import lax
from jax.experimental import pallas as pl
from jax.experimental.pallas import tpu as pltpu
from jax.sharding import PartitionSpec as P

BS = 64
KB = 32
NP = 16
W = 1024
MIB = 1 << 20
Y_GROUPS = [list(range(8)), list(range(8, 16))]


def spread(mask, width):
    count = mask.shape[0]
    lane = lax.broadcasted_iota(jnp.int32, (count, width), 1) // BS
    entry = lax.broadcasted_iota(jnp.int32, (count, width), 0)
    chosen = jnp.where(lane == entry, 1.0, 0.0).astype(jnp.bfloat16)
    return product(mask.astype(jnp.float32).astype(jnp.bfloat16), chosen)


def load(src, dst, chunk, sem):
    rows = pl.ds(chunk * (src.shape[0] // 8), src.shape[0] // 8)
    return pltpu.make_async_copy(src.at[rows], dst.at[rows], sem)


def prep(ids, kdist, mask_a, at, mask_b, bmat, to_y, a_z, x0, x1, x2, x3, b_z,
         wide_a, held_a, wide_b, held_b, in_sems, sems):
    row_id, col_id = ids[0], ids[1]
    a_half = row_id // 8
    b_half, here = col_id // 4, col_id % 4
    to_x = (x0, x1, x2, x3)
    for n in range(8):
        load(bmat, held_b, n, in_sems.at[8 + n]).start()
    for n in range(8):
        load(at, held_a, n, in_sems.at[n]).start()
    wide_b[...] = spread(mask_b[...], W)
    wide_a[...] = spread(mask_a[...].T, 2 * W)

    for block in range(2 * KB):
        if block % 8 == 0:
            load(bmat, held_b, block // 8, in_sems.at[8 + block // 8]).wait()
        gain = wide_b[block:block + 1, :].astype(jnp.bfloat16)
        rows = pl.ds(block * BS, BS)
        held_b[rows, :] = held_b[rows, :] * gain
        pos = kdist[col_id * 2 * KB + block]
        inner = pl.ds(pl.multiple_of((pos % KB - 4 * col_id) * BS, BS), BS)
        tile = (pos // KB - row_id + NP) % NP
        src = held_b.at[rows, :]
        near = (tile - 8 * b_half + NP) % NP
        far = (near + 8) % NP
        odd = tile % 2 == 1
        even = tile % 2 == 0
        first = (jnp.where(odd, tile, near) // 2 - here + 8) % 4
        kind = jnp.where(odd, jnp.where(tile // 8 == b_half, 1, 3), 0)
        second = (near // 2 - 1 - here + 8) % 4

        def send(hop, kind):
            def to(n):
                def run():
                    pltpu.make_async_copy(src, to_x[n].at[kind, inner, :], sems.at[2 + n]).start()

                return run

            lax.cond(hop < 2, lambda: lax.cond(hop == 0, to(0), to(1)), lambda: lax.cond(hop == 2, to(2), to(3)))

        @pl.when(odd | (near < 8))
        def _():
            send(first, kind)

        @pl.when(even & (near > 0) & (near <= 8))
        def _():
            send(second, 2)

        @pl.when(even & (far <= 8))
        def _():
            pltpu.make_async_copy(src, b_z.at[far // 2, inner, :], sems.at[6]).start()

    for block in range(KB):
        if block % 4 == 0:
            load(at, held_a, block // 4, in_sems.at[block // 4]).wait()
        gain = wide_a[block:block + 1, :].astype(jnp.bfloat16)
        rows = pl.ds(block * BS, BS)
        held_a[rows, :] = held_a[rows, :] * gain
        pos = kdist[row_id * KB + block]
        slot = (pos % KB - 2 * row_id) * BS
        inner = pl.ds(pl.multiple_of(slot, BS), BS)
        for t in range(2):
            tile = (pos // KB - 2 * col_id - t + 2 * NP) % NP
            cols = pl.ds(t * W, W)
            src = held_a.at[rows, cols]
            near = (tile - 8 * a_half + NP) % NP
            far = (near + 8) % NP
            odd = tile % 2 == 1
            even = tile % 2 == 0
            first = jnp.where(odd, tile // 2 % 4 * 2 + t, near)
            first_row = jnp.where(odd, jnp.where(tile // 8 == a_half, 256, 384), t * 128) + slot

            @pl.when(odd | (near < 8))
            def _():
                dst = to_y.at[first, pl.ds(pl.multiple_of(first_row, BS), BS), :]
                pltpu.make_async_copy(src, dst, sems.at[0]).start()

            @pl.when(even & (near > 0) & (near <= 8))
            def _():
                dst = to_y.at[near - 1, pl.ds(pl.multiple_of(t * 128 + slot, BS), BS), :]
                pltpu.make_async_copy(src, dst, sems.at[0]).start()

            @pl.when(even & (far <= 8))
            def _():
                pltpu.make_async_copy(src, a_z.at[far // 2, inner, cols], sems.at[1]).start()

    for n, ref in enumerate((to_y, a_z, x0, x1, x2, x3, b_z)):
        pltpu.make_async_copy(ref, ref, sems.at[n]).wait()


CONTRACT = (((0,), (0,)), ((), ()))


def product(left, right):
    return lax.dot_general(left, right, CONTRACT, preferred_element_type=jnp.float32)


def multiply(ids, near_a, e_far, o_near, o_cross, o_swap, r0, r1, r2, r3, p0, p1, p2, p3,
             out, left_out, left_v, b_v, sems, out_sem):
    row_id, col_id = ids[0], ids[1]
    core = row_id % 2
    a_half = row_id // 8
    b_half, here = col_id // 4, col_id % 4
    copies = []

    def fetch(src, dst):
        copy = pltpu.make_async_copy(src, dst, sems.at[len(copies)])
        copy.start()
        copies.append(copy)

    def group(which):
        return pl.ds(pl.multiple_of(which * W, W), W)

    sources = pl.ds(0, 8)
    a_near = pl.ds(pl.multiple_of(a_half * 8, 8), 8)
    a_far = pl.ds(pl.multiple_of(8 - a_half * 8, 8), 8)
    fetch(near_a.at[sources, pl.ds(pl.multiple_of(core * 128, 128), 128)], left_v.at[0, core, a_near])
    fetch(near_a.at[sources, pl.ds(pl.multiple_of(128 - core * 128, 128), 128)], left_v.at[1, 1 - core, a_near])
    fetch(near_a.at[sources, pl.ds(256, 128)], left_v.at[1, core, a_near])
    fetch(o_near, left_v.at[0, 1 - core, a_near])
    for hop, near in enumerate((r0, r1, r2, r3)):
        place = (here - hop + 4) % 4
        fetch(near.at[pl.ds(0, 3)], b_v.at[:, pl.ds(pl.multiple_of((b_half * 4 + place) * 256, 256), 256)])
    for hop, far in enumerate((p0, p1, p2, p3)):
        place = (here - hop + 4) % 4
        rows = pl.ds(pl.multiple_of(((1 - b_half) * 4 + place) * 256, 256), 256)
        base = here if hop == 0 else 0
        fetch(far.at[base], b_v.at[0, rows])
        fetch(far.at[base + 1], b_v.at[2, rows])
    fetch(e_far.at[sources, :, group(core)], left_v.at[0, core, a_far])
    fetch(e_far.at[sources, :, group(1 - core)], left_v.at[1, 1 - core, a_far])
    fetch(o_cross, left_v.at[1, core, a_far])
    fetch(o_swap, left_v.at[0, 1 - core, a_far])
    for copy in copies:
        copy.wait()
    later = []
    for t in range(2):
        for hop in range(4):
            place = (here - hop + 4) % 4
            part = pltpu.make_async_copy(
                left_v.at[1, t, pl.ds((1 - b_half) * 8 + place * 2, 2)],
                left_out.at[t, pl.ds(hop * 2, 2)], out_sem.at[t * 4 + hop])
            part.start()
            later.append(part)
    near_rows = pl.ds(pl.multiple_of(b_half * W, W), W)
    near_pieces = pl.ds(pl.multiple_of(b_half * 8, 8), 8)
    for t in range(2):
        for m in range(4):
            cols = slice(m * 256, (m + 1) * 256)
            total = product(left_v[0, t, :, :, cols].reshape(2 * W, 256), b_v[2 * t])
            total += product(left_v[1, t, near_pieces, :, cols].reshape(W, 256), b_v[1, near_rows])
            out[t * W + m * 256:t * W + (m + 1) * 256, :] = total
    for part in later:
        part.wait()


def finish(filt, part, left, right, out, wide, done, sems):
    wide[...] = spread(filt[...], W)
    copies = []
    for t in range(2):
        for m in range(4):
            first = t * W + m * 256
            if len(copies) >= 2:
                copies[-2].wait()
            spot = done.at[len(copies) % 2]
            total = product(left[t, :, :, m * 256:(m + 1) * 256].reshape(W, 256), right[...].reshape(W, W))
            total += part[first:first + 256, :]
            for i in range(4):
                rows = slice(i * BS, (i + 1) * BS)
                block = first // BS + i
                spot[rows, :] = total[rows, :] * wide[block:block + 1, :]
            copies.append(pltpu.make_async_copy(spot, out.at[pl.ds(first, 256)], sems.at[len(copies) % 2]))
            copies[-1].start()
    for copy in copies[-2:]:
        copy.wait()


SMEM = pl.BlockSpec(memory_space=pltpu.SMEM)
ANY = pl.BlockSpec(memory_space=pl.ANY)
HBM = pl.BlockSpec(memory_space=pltpu.HBM)
VMEM = pl.BlockSpec(memory_space=pltpu.VMEM)


def bf16(*shape):
    return pltpu.HBM(shape, jnp.bfloat16)


def in_hbm(*values):
    return [pltpu.with_memory_space_constraint(value, pltpu.HBM) for value in values]


def in_vmem(*values):
    return [pltpu.with_memory_space_constraint(value, pltpu.VMEM) for value in values]


def on_device(at, bmat, mask_a, mask_b, filt, kdist):
    row_id = lax.axis_index("row")
    col_id = lax.axis_index("col")
    ids = jnp.stack([row_id, col_id]).astype(jnp.int32)
    here = col_id % 4

    def swap_z_hi(value):
        return lax.ppermute(value, "row", [(i, i ^ 8) for i in range(16)])

    def swap_z_lo(value):
        return lax.ppermute(value, "col", [(i, i ^ 4) for i in range(8)])

    def swap_core(value):
        return lax.ppermute(value, "row", [(i, i ^ 1) for i in range(16)])

    def along_x(value, hop):
        return lax.ppermute(value, "col", [(i, i // 4 * 4 + (i % 4 + hop) % 4) for i in range(8)])

    def along_y(value):
        return lax.all_to_all(value, "row", 0, 0, axis_index_groups=Y_GROUPS, tiled=True)

    a_y, a_z, x0, x1, x2, x3, b_z = pl.pallas_call(
        prep,
        out_shape=[bf16(8, 512, W), bf16(5, 128, 2 * W)] + [bf16(4, 256, W)] * 4 + [bf16(5, 256, W)],
        in_specs=[SMEM, SMEM, VMEM, HBM, VMEM, HBM],
        out_specs=[HBM] * 7,
        scratch_shapes=[pltpu.VMEM((32, 2 * W), jnp.float32), pltpu.VMEM((2048, 2 * W), jnp.bfloat16),
                        pltpu.VMEM((64, W), jnp.float32), pltpu.VMEM((4096, W), jnp.bfloat16),
                        pltpu.SemaphoreType.DMA((16,)), pltpu.SemaphoreType.DMA((7,))],
        compiler_params=pltpu.CompilerParams(vmem_limit_bytes=32 * MIB),
        name="prep",
    )(ids, kdist, mask_a, *in_hbm(at), mask_b.T, *in_hbm(bmat))

    b_cross = swap_z_lo(b_z)
    r1, r3 = along_x(x1, 1), along_x(x3, 3)
    x2, r1, r3 = lax.optimization_barrier((x2, r1, r3))
    r2 = along_x(x2, 2)
    a_cross = swap_z_hi(a_z)
    near_a = along_y(a_y)

    o_send = near_a[:, 384:]
    q_send = jnp.concatenate([v[3:4] for v in (x0, r1, r2, r3)], axis=0)
    a_cross, b_cross, near_a, o_send, q_send = lax.optimization_barrier((a_cross, b_cross, near_a, o_send, q_send))
    o_cross = swap_z_hi(o_send)
    o_near = swap_core(near_a[:, 256:384])

    far = [lax.dynamic_slice_in_dim(b_cross, (here + hop) % 4, 2, 0) for hop in range(1, 4)]
    a_cross, *far = lax.optimization_barrier((a_cross, *far))
    p1, p2, p3 = along_x(far[0], 1), along_x(far[1], 2), along_x(far[2], 3)
    e_far = along_y(jnp.stack([a_cross[:4], a_cross[1:]], axis=1).reshape(8, 128, 2 * W))

    q_send, o_cross, p1, p2, p3 = lax.optimization_barrier((q_send, o_cross, p1, p2, p3))
    q = swap_z_lo(q_send)
    o_swap = swap_core(o_cross)

    part, left = pl.pallas_call(
        multiply,
        out_shape=[pltpu.VMEM((2 * W, W), jnp.float32), pltpu.VMEM((2, 8, 128, W), jnp.bfloat16)],
        in_specs=[SMEM] + [ANY] * 13,
        out_specs=[VMEM, VMEM],
        scratch_shapes=[pltpu.VMEM((2, 2, 16, 128, W), jnp.bfloat16), pltpu.VMEM((3, 2048, W), jnp.bfloat16),
                        pltpu.SemaphoreType.DMA((20,)), pltpu.SemaphoreType.DMA((8,))],
        compiler_params=pltpu.CompilerParams(vmem_limit_bytes=38 * MIB),
        name="multiply",
    )(ids, *in_hbm(near_a, e_far, o_near, o_cross, o_swap, x0, r1, r2, r3, b_cross, p1, p2, p3))
    return pl.pallas_call(
        finish,
        out_shape=jax.ShapeDtypeStruct((2 * W, W), jnp.float32),
        in_specs=[VMEM] * 4,
        out_specs=HBM,
        scratch_shapes=[pltpu.VMEM((32, W), jnp.float32), pltpu.VMEM((2, 256, W), jnp.float32),
                        pltpu.SemaphoreType.DMA((2,))],
        compiler_params=pltpu.CompilerParams(vmem_limit_bytes=8 * MIB),
        name="finish",
    )(filt.T, *in_vmem(part, left, q))


def solution(mesh):
    in_specs = (
        P("row", "col"),
        P("col", "row"),
        P("row", "col"),
        P("col", "row"),
        P("col", "row"),
        P(),
    )
    out_specs = P("col", "row")
    return jax.shard_map(
        on_device, mesh=mesh, in_specs=in_specs, out_specs=out_specs, check_vma=False
    )
```

```python
import jax
import jax.numpy as jnp
from jax import lax
from jax.experimental import pallas as pl
from jax.experimental.pallas import tpu as pltpu
from jax.sharding import PartitionSpec as P

BS = 64
KB = 32
NP = 16
W = 1024
MIB = 1 << 20
Y_GROUPS = [list(range(8)), list(range(8, 16))]


def spread(mask, width):
    count = mask.shape[0]
    lane = lax.broadcasted_iota(jnp.int32, (count, width), 1) // BS
    entry = lax.broadcasted_iota(jnp.int32, (count, width), 0)
    chosen = jnp.where(lane == entry, 1.0, 0.0).astype(jnp.bfloat16)
    return product(mask.astype(jnp.float32).astype(jnp.bfloat16), chosen)


def load(src, dst, chunk, sem):
    rows = pl.ds(chunk * (src.shape[0] // 8), src.shape[0] // 8)
    return pltpu.make_async_copy(src.at[rows], dst.at[rows], sem)


def prep_a(ids, kdist, mask_a, at, to_y, a_z, to_odd, wide_a, held_a, in_sems, sems):
    row_id, col_id = ids[0], ids[1]
    a_half = row_id // 8
    for n in range(8):
        load(at, held_a, n, in_sems.at[n]).start()
    wide_a[...] = spread(mask_a[...].T, 2 * W)
    for block in range(KB):
        if block % 4 == 0:
            load(at, held_a, block // 4, in_sems.at[block // 4]).wait()
        gain = wide_a[block:block + 1, :].astype(jnp.bfloat16)
        rows = pl.ds(block * BS, BS)
        held_a[rows, :] = held_a[rows, :] * gain
        pos = kdist[row_id * KB + block]
        slot = (pos % KB - 2 * row_id) * BS
        inner = pl.ds(pl.multiple_of(slot, BS), BS)
        for t in range(2):
            tile = (pos // KB - 2 * col_id - t + 2 * NP) % NP
            cols = pl.ds(t * W, W)
            src = held_a.at[rows, cols]
            near = (tile - 8 * a_half + NP) % NP
            far = (near + 8) % NP
            odd = tile % 2 == 1
            even = tile % 2 == 0
            first = jnp.where(odd, tile // 2 % 4 * 2 + t, near)
            first_row = jnp.where(odd, 256, t * 128) + slot

            @pl.when(odd & (near >= 8))
            def _():
                pltpu.make_async_copy(src, to_odd.at[first, inner, :], sems.at[2]).start()

            @pl.when(near < 8)
            def _():
                dst = to_y.at[first, pl.ds(pl.multiple_of(first_row, BS), BS), :]
                pltpu.make_async_copy(src, dst, sems.at[0]).start()

            @pl.when(even & (near > 0) & (near <= 8))
            def _():
                dst = to_y.at[near - 1, pl.ds(pl.multiple_of(t * 128 + slot, BS), BS), :]
                pltpu.make_async_copy(src, dst, sems.at[0]).start()

            @pl.when(even & (far <= 8))
            def _():
                pltpu.make_async_copy(src, a_z.at[far // 2, inner, cols], sems.at[1]).start()

    for n, ref in enumerate((to_y, a_z, to_odd)):
        pltpu.make_async_copy(ref, ref, sems.at[n]).wait()


def prep_b(ids, kdist, mask_b, bmat, x0, x1, x2, x3, b_z, wide_b, held_b, in_sems, sems):
    row_id, col_id = ids[0], ids[1]
    b_half, here = col_id // 4, col_id % 4
    to_x = (x0, x1, x2, x3)
    for n in range(8):
        load(bmat, held_b, n, in_sems.at[n]).start()
    wide_b[...] = spread(mask_b[...], W)
    for block in range(2 * KB):
        if block % 8 == 0:
            load(bmat, held_b, block // 8, in_sems.at[block // 8]).wait()
        gain = wide_b[block:block + 1, :].astype(jnp.bfloat16)
        rows = pl.ds(block * BS, BS)
        held_b[rows, :] = held_b[rows, :] * gain
        pos = kdist[col_id * 2 * KB + block]
        inner = pl.ds(pl.multiple_of((pos % KB - 4 * col_id) * BS, BS), BS)
        tile = (pos // KB - row_id + NP) % NP
        src = held_b.at[rows, :]
        near = (tile - 8 * b_half + NP) % NP
        far = (near + 8) % NP
        odd = tile % 2 == 1
        even = tile % 2 == 0
        first = (jnp.where(odd, tile, near) // 2 - here + 8) % 4
        kind = jnp.where(odd, jnp.where(tile // 8 == b_half, 1, 3), 0)
        second = (near // 2 - 1 - here + 8) % 4

        def send(hop, kind):
            def to(n):
                def run():
                    pltpu.make_async_copy(src, to_x[n].at[kind, inner, :], sems.at[n]).start()

                return run

            lax.cond(hop < 2, lambda: lax.cond(hop == 0, to(0), to(1)), lambda: lax.cond(hop == 2, to(2), to(3)))

        @pl.when(odd | (near < 8))
        def _():
            send(first, kind)

        @pl.when(even & (near > 0) & (near <= 8))
        def _():
            send(second, 2)

        @pl.when(even & (far <= 8))
        def _():
            pltpu.make_async_copy(src, b_z.at[far // 2, inner, :], sems.at[4]).start()

    for n, ref in enumerate((x0, x1, x2, x3, b_z)):
        pltpu.make_async_copy(ref, ref, sems.at[n]).wait()


CONTRACT = (((0,), (0,)), ((), ()))


def product(left, right):
    return lax.dot_general(left, right, CONTRACT, preferred_element_type=jnp.float32)


def multiply(ids, near_a, e_far, o_near, o_cross, o_swap, r0, r1, r2, r3, p0, p1, p2, p3,
             out, left_out, left_v, b_v, sems, out_sem):
    row_id, col_id = ids[0], ids[1]
    core = row_id % 2
    a_half = row_id // 8
    b_half, here = col_id // 4, col_id % 4
    copies = []

    def fetch(src, dst):
        copy = pltpu.make_async_copy(src, dst, sems.at[len(copies)])
        copy.start()
        copies.append(copy)

    def group(which):
        return pl.ds(pl.multiple_of(which * W, W), W)

    sources = pl.ds(0, 8)
    a_near = pl.ds(pl.multiple_of(a_half * 8, 8), 8)
    a_far = pl.ds(pl.multiple_of(8 - a_half * 8, 8), 8)
    fetch(near_a.at[sources, pl.ds(pl.multiple_of(core * 128, 128), 128)], left_v.at[0, core, a_near])
    fetch(near_a.at[sources, pl.ds(pl.multiple_of(128 - core * 128, 128), 128)], left_v.at[1, 1 - core, a_near])
    fetch(near_a.at[sources, pl.ds(256, 128)], left_v.at[1, core, a_near])
    fetch(o_near, left_v.at[0, 1 - core, a_near])
    for hop, near in enumerate((r0, r1, r2, r3)):
        place = (here - hop + 4) % 4
        fetch(near.at[pl.ds(0, 3)], b_v.at[:, pl.ds(pl.multiple_of((b_half * 4 + place) * 256, 256), 256)])
    for hop, far in enumerate((p0, p1, p2, p3)):
        place = (here - hop + 4) % 4
        rows = pl.ds(pl.multiple_of(((1 - b_half) * 4 + place) * 256, 256), 256)
        base = here if hop == 0 else 0
        fetch(far.at[base], b_v.at[0, rows])
        fetch(far.at[base + 1], b_v.at[2, rows])
    fetch(e_far.at[sources, :, group(core)], left_v.at[0, core, a_far])
    fetch(e_far.at[sources, :, group(1 - core)], left_v.at[1, 1 - core, a_far])
    fetch(o_cross, left_v.at[1, core, a_far])
    fetch(o_swap, left_v.at[0, 1 - core, a_far])
    for copy in copies:
        copy.wait()
    later = []
    for t in range(2):
        for hop in range(4):
            place = (here - hop + 4) % 4
            part = pltpu.make_async_copy(
                left_v.at[1, t, pl.ds((1 - b_half) * 8 + place * 2, 2)],
                left_out.at[t, pl.ds(hop * 2, 2)], out_sem.at[t * 4 + hop])
            part.start()
            later.append(part)
    near_rows = pl.ds(pl.multiple_of(b_half * W, W), W)
    near_pieces = pl.ds(pl.multiple_of(b_half * 8, 8), 8)
    for t in range(2):
        for m in range(4):
            cols = slice(m * 256, (m + 1) * 256)
            total = product(left_v[0, t, :, :, cols].reshape(2 * W, 256), b_v[2 * t])
            total += product(left_v[1, t, near_pieces, :, cols].reshape(W, 256), b_v[1, near_rows])
            out[t * W + m * 256:t * W + (m + 1) * 256, :] = total
    for part in later:
        part.wait()


def finish(filt, part, left, right, out, wide, done, sems):
    wide[...] = spread(filt[...], W)
    copies = []
    for t in range(2):
        for m in range(4):
            first = t * W + m * 256
            if len(copies) >= 2:
                copies[-2].wait()
            spot = done.at[len(copies) % 2]
            total = product(left[t, :, :, m * 256:(m + 1) * 256].reshape(W, 256), right[...].reshape(W, W))
            total += part[first:first + 256, :]
            for i in range(4):
                rows = slice(i * BS, (i + 1) * BS)
                block = first // BS + i
                spot[rows, :] = total[rows, :] * wide[block:block + 1, :]
            copies.append(pltpu.make_async_copy(spot, out.at[pl.ds(first, 256)], sems.at[len(copies) % 2]))
            copies[-1].start()
    for copy in copies[-2:]:
        copy.wait()


SMEM = pl.BlockSpec(memory_space=pltpu.SMEM)
ANY = pl.BlockSpec(memory_space=pl.ANY)
HBM = pl.BlockSpec(memory_space=pltpu.HBM)
VMEM = pl.BlockSpec(memory_space=pltpu.VMEM)


def bf16(*shape):
    return pltpu.HBM(shape, jnp.bfloat16)


def in_hbm(*values):
    return [pltpu.with_memory_space_constraint(value, pltpu.HBM) for value in values]


def in_vmem(*values):
    return [pltpu.with_memory_space_constraint(value, pltpu.VMEM) for value in values]


def on_device(at, bmat, mask_a, mask_b, filt, kdist):
    row_id = lax.axis_index("row")
    col_id = lax.axis_index("col")
    ids = jnp.stack([row_id, col_id]).astype(jnp.int32)
    here = col_id % 4

    def swap_z_hi(value):
        return lax.ppermute(value, "row", [(i, i ^ 8) for i in range(16)])

    def swap_z_lo(value):
        return lax.ppermute(value, "col", [(i, i ^ 4) for i in range(8)])

    def swap_core(value):
        return lax.ppermute(value, "row", [(i, i ^ 1) for i in range(16)])

    def along_x(value, hop):
        return lax.ppermute(value, "col", [(i, i // 4 * 4 + (i % 4 + hop) % 4) for i in range(8)])

    def along_y(value):
        return lax.all_to_all(value, "row", 0, 0, axis_index_groups=Y_GROUPS, tiled=True)

    x0, x1, x2, x3, b_z = pl.pallas_call(
        prep_b,
        out_shape=[bf16(4, 256, W)] * 4 + [bf16(5, 256, W)],
        in_specs=[SMEM, SMEM, VMEM, HBM],
        out_specs=[HBM] * 5,
        scratch_shapes=[pltpu.VMEM((64, W), jnp.float32), pltpu.VMEM((4096, W), jnp.bfloat16),
                        pltpu.SemaphoreType.DMA((8,)), pltpu.SemaphoreType.DMA((5,))],
        compiler_params=pltpu.CompilerParams(vmem_limit_bytes=24 * MIB),
        name="prep_b",
    )(ids, kdist, mask_b.T, *in_hbm(bmat))

    b_cross = swap_z_lo(b_z)
    r1, r3 = along_x(x1, 1), along_x(x3, 3)
    x2, r1, r3 = lax.optimization_barrier((x2, r1, r3))
    r2 = along_x(x2, 2)
    at, b_z = lax.optimization_barrier((at, b_z))
    a_y, a_z, a_odd = pl.pallas_call(
        prep_a,
        out_shape=[bf16(8, 384, W), bf16(5, 128, 2 * W), bf16(8, 128, W)],
        in_specs=[SMEM, SMEM, VMEM, HBM],
        out_specs=[HBM] * 3,
        scratch_shapes=[pltpu.VMEM((32, 2 * W), jnp.float32), pltpu.VMEM((2048, 2 * W), jnp.bfloat16),
                        pltpu.SemaphoreType.DMA((8,)), pltpu.SemaphoreType.DMA((3,))],
        compiler_params=pltpu.CompilerParams(vmem_limit_bytes=24 * MIB),
        name="prep_a",
    )(ids, kdist, mask_a, *in_hbm(at))
    o_send = along_y(a_odd)
    a_y, o_send = lax.optimization_barrier((a_y, o_send))
    near_a = along_y(a_y)
    a_z, b_cross, r1, r3 = lax.optimization_barrier((a_z, b_cross, r1, r3))
    a_cross = swap_z_hi(a_z)
    far = [lax.dynamic_slice_in_dim(b_cross, (here + hop) % 4, 2, 0) for hop in range(1, 4)]
    p1, p3 = along_x(far[0], 1), along_x(far[2], 3)

    o_send, p2_send, a_cross, p1, p3 = lax.optimization_barrier((o_send, far[1], a_cross, p1, p3))
    o_cross = swap_z_hi(o_send)
    p2 = along_x(p2_send, 2)
    e_far = along_y(jnp.stack([a_cross[:4], a_cross[1:]], axis=1).reshape(8, 128, 2 * W))
    o_near = swap_core(near_a[:, 256:])

    q_send = jnp.concatenate([v[3:4] for v in (x0, r1, r2, r3)], axis=0)
    q_send, o_cross, p2 = lax.optimization_barrier((q_send, o_cross, p2))
    q = swap_z_lo(q_send)
    o_swap = swap_core(o_cross)

    part, left = pl.pallas_call(
        multiply,
        out_shape=[pltpu.VMEM((2 * W, W), jnp.float32), pltpu.VMEM((2, 8, 128, W), jnp.bfloat16)],
        in_specs=[SMEM] + [ANY] * 13,
        out_specs=[VMEM, VMEM],
        scratch_shapes=[pltpu.VMEM((2, 2, 16, 128, W), jnp.bfloat16), pltpu.VMEM((3, 2048, W), jnp.bfloat16),
                        pltpu.SemaphoreType.DMA((20,)), pltpu.SemaphoreType.DMA((8,))],
        compiler_params=pltpu.CompilerParams(vmem_limit_bytes=38 * MIB),
        name="multiply",
    )(ids, *in_hbm(near_a, e_far, o_near, o_cross, o_swap, x0, r1, r2, r3, b_cross, p1, p2, p3))
    return pl.pallas_call(
        finish,
        out_shape=jax.ShapeDtypeStruct((2 * W, W), jnp.float32),
        in_specs=[VMEM] * 4,
        out_specs=HBM,
        scratch_shapes=[pltpu.VMEM((32, W), jnp.float32), pltpu.VMEM((2, 256, W), jnp.float32),
                        pltpu.SemaphoreType.DMA((2,))],
        compiler_params=pltpu.CompilerParams(vmem_limit_bytes=8 * MIB),
        name="finish",
    )(filt.T, *in_vmem(part, left, q))


def solution(mesh):
    in_specs = (
        P("row", "col"),
        P("col", "row"),
        P("row", "col"),
        P("col", "row"),
        P("col", "row"),
        P(),
    )
    out_specs = P("col", "row")
    return jax.shard_map(
        on_device, mesh=mesh, in_specs=in_specs, out_specs=out_specs, check_vma=False
    )
```

```python
import jax
import jax.numpy as jnp
from jax import lax
from jax.experimental import pallas as pl
from jax.experimental.pallas import tpu as pltpu
from jax.sharding import PartitionSpec as P

BS = 64
KB = 32
NP = 16
W = 1024
MIB = 1 << 20
Y_GROUPS = [list(range(8)), list(range(8, 16))]


def spread(mask, width):
    count = mask.shape[0]
    lane = lax.broadcasted_iota(jnp.int32, (count, width), 1) // BS
    entry = lax.broadcasted_iota(jnp.int32, (count, width), 0)
    chosen = jnp.where(lane == entry, 1.0, 0.0).astype(jnp.bfloat16)
    return product(mask.astype(jnp.float32).astype(jnp.bfloat16), chosen)


def load(src, dst, chunk, sem):
    rows = pl.ds(chunk * (src.shape[0] // 8), src.shape[0] // 8)
    return pltpu.make_async_copy(src.at[rows], dst.at[rows], sem)


def prep(ids, kdist, mask_a, at, mask_b, bmat, to_y, a_z, x0, x1, x2, x3, b_z,
         wide_a, held_a, wide_b, held_b, in_sems, sems):
    row_id, col_id = ids[0], ids[1]
    a_half = row_id // 8
    b_half, here = col_id // 4, col_id % 4
    to_x = (x0, x1, x2, x3)
    for n in range(8):
        load(bmat, held_b, n, in_sems.at[8 + n]).start()
    for n in range(8):
        load(at, held_a, n, in_sems.at[n]).start()
    wide_b[...] = spread(mask_b[...], W)
    wide_a[...] = spread(mask_a[...].T, 2 * W)

    for block in range(2 * KB):
        if block % 8 == 0:
            load(bmat, held_b, block // 8, in_sems.at[8 + block // 8]).wait()
        gain = wide_b[block:block + 1, :].astype(jnp.bfloat16)
        rows = pl.ds(block * BS, BS)
        held_b[rows, :] = held_b[rows, :] * gain
        pos = kdist[col_id * 2 * KB + block]
        inner = pl.ds(pl.multiple_of((pos % KB - 4 * col_id) * BS, BS), BS)
        tile = (pos // KB - row_id + NP) % NP
        src = held_b.at[rows, :]
        near = (tile - 8 * b_half + NP) % NP
        far = (near + 8) % NP
        odd = tile % 2 == 1
        even = tile % 2 == 0
        first = (jnp.where(odd, tile, near) // 2 - here + 8) % 4
        kind = jnp.where(odd, jnp.where(tile // 8 == b_half, 1, 3), 0)
        second = (near // 2 - 1 - here + 8) % 4

        def send(hop, kind):
            def to(n):
                def run():
                    pltpu.make_async_copy(src, to_x[n].at[kind, inner, :], sems.at[2 + n]).start()

                return run

            lax.cond(hop < 2, lambda: lax.cond(hop == 0, to(0), to(1)), lambda: lax.cond(hop == 2, to(2), to(3)))

        @pl.when(odd | (near < 8))
        def _():
            send(first, kind)

        @pl.when(even & (near > 0) & (near <= 8))
        def _():
            send(second, 2)

        @pl.when(even & (far <= 8))
        def _():
            pltpu.make_async_copy(src, b_z.at[far // 2, inner, :], sems.at[6]).start()

    for block in range(KB):
        if block % 4 == 0:
            load(at, held_a, block // 4, in_sems.at[block // 4]).wait()
        gain = wide_a[block:block + 1, :].astype(jnp.bfloat16)
        rows = pl.ds(block * BS, BS)
        held_a[rows, :] = held_a[rows, :] * gain
        pos = kdist[row_id * KB + block]
        slot = (pos % KB - 2 * row_id) * BS
        inner = pl.ds(pl.multiple_of(slot, BS), BS)
        for t in range(2):
            tile = (pos // KB - 2 * col_id - t + 2 * NP) % NP
            cols = pl.ds(t * W, W)
            src = held_a.at[rows, cols]
            near = (tile - 8 * a_half + NP) % NP
            far = (near + 8) % NP
            odd = tile % 2 == 1
            even = tile % 2 == 0
            first = jnp.where(odd, tile // 2 % 4 * 2 + t, near)
            first_row = jnp.where(odd, jnp.where(tile // 8 == a_half, 256, 384), t * 128) + slot

            @pl.when(odd | (near < 8))
            def _():
                dst = to_y.at[first, pl.ds(pl.multiple_of(first_row, BS), BS), :]
                pltpu.make_async_copy(src, dst, sems.at[0]).start()

            @pl.when(even & (near > 0) & (near <= 8))
            def _():
                dst = to_y.at[near - 1, pl.ds(pl.multiple_of(t * 128 + slot, BS), BS), :]
                pltpu.make_async_copy(src, dst, sems.at[0]).start()

            @pl.when(even & (far <= 8))
            def _():
                pltpu.make_async_copy(src, a_z.at[far // 2, inner, cols], sems.at[1]).start()

    for n, ref in enumerate((to_y, a_z, x0, x1, x2, x3, b_z)):
        pltpu.make_async_copy(ref, ref, sems.at[n]).wait()


CONTRACT = (((0,), (0,)), ((), ()))


def product(left, right):
    return lax.dot_general(left, right, CONTRACT, preferred_element_type=jnp.float32)


def multiply(ids, near_a, e_far, o_near, o_cross, o_swap, r0, r1, r2, r3, p0, p1, p2, p3,
             out, left_out, left_v, b_v, sems, out_sem):
    row_id, col_id = ids[0], ids[1]
    core = row_id % 2
    a_half = row_id // 8
    b_half, here = col_id // 4, col_id % 4
    copies = []

    def fetch(src, dst):
        copy = pltpu.make_async_copy(src, dst, sems.at[len(copies)])
        copy.start()
        copies.append(copy)

    def group(which):
        return pl.ds(pl.multiple_of(which * W, W), W)

    sources = pl.ds(0, 8)
    a_near = pl.ds(pl.multiple_of(a_half * 8, 8), 8)
    a_far = pl.ds(pl.multiple_of(8 - a_half * 8, 8), 8)
    for hop, near in enumerate((r0, r1, r2, r3)):
        place = (here - hop + 4) % 4
        fetch(near.at[pl.ds(0, 3)], b_v.at[:, pl.ds(pl.multiple_of((b_half * 4 + place) * 256, 256), 256)])
    for hop, far in enumerate((p0, p1, p2, p3)):
        place = (here - hop + 4) % 4
        rows = pl.ds(pl.multiple_of(((1 - b_half) * 4 + place) * 256, 256), 256)
        base = here if hop == 0 else 0
        fetch(far.at[base], b_v.at[0, rows])
        fetch(far.at[base + 1], b_v.at[2, rows])
    fetch(near_a.at[sources, pl.ds(pl.multiple_of(core * 128, 128), 128)], left_v.at[0, core, a_near])
    fetch(e_far.at[sources, :, group(core)], left_v.at[0, core, a_far])
    fetch(near_a.at[sources, pl.ds(256, 128)], left_v.at[1, core, a_near])
    fetch(o_cross, left_v.at[1, core, a_far])
    ready = len(copies)
    fetch(o_near, left_v.at[0, 1 - core, a_near])
    fetch(o_swap, left_v.at[0, 1 - core, a_far])
    fetch(near_a.at[sources, pl.ds(pl.multiple_of(128 - core * 128, 128), 128)], left_v.at[1, 1 - core, a_near])
    fetch(e_far.at[sources, :, group(1 - core)], left_v.at[1, 1 - core, a_far])
    later = []
    near_rows = pl.ds(pl.multiple_of(b_half * W, W), W)
    near_pieces = pl.ds(pl.multiple_of(b_half * 8, 8), 8)
    for turn, t in enumerate((core, 1 - core)):
        for copy in copies[turn * ready:ready + turn * 4]:
            copy.wait()
        for hop in range(4):
            place = (here - hop + 4) % 4
            part = pltpu.make_async_copy(
                left_v.at[1, t, pl.ds((1 - b_half) * 8 + place * 2, 2)],
                left_out.at[t, pl.ds(hop * 2, 2)], out_sem.at[turn * 4 + hop])
            part.start()
            later.append(part)
        for m in range(4):
            cols = slice(m * 256, (m + 1) * 256)
            total = product(left_v[0, t, :, :, cols].reshape(2 * W, 256), b_v[2 * t])
            total += product(left_v[1, t, near_pieces, :, cols].reshape(W, 256), b_v[1, near_rows])
            out[pl.ds(pl.multiple_of(t * W + m * 256, 256), 256), :] = total
    for part in later:
        part.wait()


def finish(filt, part, left, right, out, wide, done, sems):
    wide[...] = spread(filt[...], W)
    copies = []
    for t in range(2):
        for m in range(4):
            first = t * W + m * 256
            if len(copies) >= 2:
                copies[-2].wait()
            spot = done.at[len(copies) % 2]
            total = product(left[t, :, :, m * 256:(m + 1) * 256].reshape(W, 256), right[...].reshape(W, W))
            total += part[first:first + 256, :]
            for i in range(4):
                rows = slice(i * BS, (i + 1) * BS)
                block = first // BS + i
                spot[rows, :] = total[rows, :] * wide[block:block + 1, :]
            copies.append(pltpu.make_async_copy(spot, out.at[pl.ds(first, 256)], sems.at[len(copies) % 2]))
            copies[-1].start()
    for copy in copies[-2:]:
        copy.wait()


SMEM = pl.BlockSpec(memory_space=pltpu.SMEM)
ANY = pl.BlockSpec(memory_space=pl.ANY)
HBM = pl.BlockSpec(memory_space=pltpu.HBM)
VMEM = pl.BlockSpec(memory_space=pltpu.VMEM)


def bf16(*shape):
    return pltpu.HBM(shape, jnp.bfloat16)


def in_hbm(*values):
    return [pltpu.with_memory_space_constraint(value, pltpu.HBM) for value in values]


def in_vmem(*values):
    return [pltpu.with_memory_space_constraint(value, pltpu.VMEM) for value in values]


def on_device(at, bmat, mask_a, mask_b, filt, kdist):
    row_id = lax.axis_index("row")
    col_id = lax.axis_index("col")
    ids = jnp.stack([row_id, col_id]).astype(jnp.int32)
    here = col_id % 4

    def swap_z_hi(value):
        return lax.ppermute(value, "row", [(i, i ^ 8) for i in range(16)])

    def swap_z_lo(value):
        return lax.ppermute(value, "col", [(i, i ^ 4) for i in range(8)])

    def swap_core(value):
        return lax.ppermute(value, "row", [(i, i ^ 1) for i in range(16)])

    def along_x(value, hop):
        return lax.ppermute(value, "col", [(i, i // 4 * 4 + (i % 4 + hop) % 4) for i in range(8)])

    def along_y(value):
        return lax.all_to_all(value, "row", 0, 0, axis_index_groups=Y_GROUPS, tiled=True)

    a_y, a_z, x0, x1, x2, x3, b_z = pl.pallas_call(
        prep,
        out_shape=[bf16(8, 512, W), bf16(5, 128, 2 * W)] + [bf16(4, 256, W)] * 4 + [bf16(5, 256, W)],
        in_specs=[SMEM, SMEM, VMEM, HBM, VMEM, HBM],
        out_specs=[HBM] * 7,
        scratch_shapes=[pltpu.VMEM((32, 2 * W), jnp.float32), pltpu.VMEM((2048, 2 * W), jnp.bfloat16),
                        pltpu.VMEM((64, W), jnp.float32), pltpu.VMEM((4096, W), jnp.bfloat16),
                        pltpu.SemaphoreType.DMA((16,)), pltpu.SemaphoreType.DMA((7,))],
        compiler_params=pltpu.CompilerParams(vmem_limit_bytes=32 * MIB),
        name="prep",
    )(ids, kdist, mask_a, *in_hbm(at), mask_b.T, *in_hbm(bmat))

    b_cross = swap_z_lo(b_z)
    r1, r3 = along_x(x1, 1), along_x(x3, 3)
    x2, r1, r3 = lax.optimization_barrier((x2, r1, r3))
    r2 = along_x(x2, 2)
    a_cross = swap_z_hi(a_z)
    near_a = along_y(a_y)

    o_send = near_a[:, 384:]
    q_send = jnp.concatenate([v[3:4] for v in (x0, r1, r2, r3)], axis=0)
    a_cross, b_cross, near_a, o_send, q_send = lax.optimization_barrier((a_cross, b_cross, near_a, o_send, q_send))
    o_cross = swap_z_hi(o_send)
    o_near = swap_core(near_a[:, 256:384])

    e_far = along_y(jnp.stack([a_cross[:4], a_cross[1:]], axis=1).reshape(8, 128, 2 * W))
    far = [lax.dynamic_slice_in_dim(b_cross, (here + hop) % 4, 2, 0) for hop in range(1, 4)]
    p1, p3 = along_x(far[0], 1), along_x(far[2], 3)
    p2_send, p1, p3 = lax.optimization_barrier((far[1], p1, p3))
    p2 = along_x(p2_send, 2)

    q_send, o_cross, p1, p3 = lax.optimization_barrier((q_send, o_cross, p1, p3))
    q = swap_z_lo(q_send)
    o_swap = swap_core(o_cross)

    part, left = pl.pallas_call(
        multiply,
        out_shape=[pltpu.VMEM((2 * W, W), jnp.float32), pltpu.VMEM((2, 8, 128, W), jnp.bfloat16)],
        in_specs=[SMEM] + [ANY] * 13,
        out_specs=[VMEM, VMEM],
        scratch_shapes=[pltpu.VMEM((2, 2, 16, 128, W), jnp.bfloat16), pltpu.VMEM((3, 2048, W), jnp.bfloat16),
                        pltpu.SemaphoreType.DMA((20,)), pltpu.SemaphoreType.DMA((8,))],
        compiler_params=pltpu.CompilerParams(vmem_limit_bytes=38 * MIB),
        name="multiply",
    )(ids, *in_hbm(near_a, e_far, o_near, o_cross, o_swap, x0, r1, r2, r3, b_cross, p1, p2, p3))
    return pl.pallas_call(
        finish,
        out_shape=jax.ShapeDtypeStruct((2 * W, W), jnp.float32),
        in_specs=[VMEM] * 4,
        out_specs=HBM,
        scratch_shapes=[pltpu.VMEM((32, W), jnp.float32), pltpu.VMEM((2, 256, W), jnp.float32),
                        pltpu.SemaphoreType.DMA((2,))],
        compiler_params=pltpu.CompilerParams(vmem_limit_bytes=8 * MIB),
        name="finish",
    )(filt.T, *in_vmem(part, left, q))


def solution(mesh):
    in_specs = (
        P("row", "col"),
        P("col", "row"),
        P("row", "col"),
        P("col", "row"),
        P("col", "row"),
        P(),
    )
    out_specs = P("col", "row")
    return jax.shard_map(
        on_device, mesh=mesh, in_specs=in_specs, out_specs=out_specs, check_vma=False
    )
```

```python
import jax
import jax.numpy as jnp
from jax import lax
from jax.experimental import pallas as pl
from jax.experimental.pallas import tpu as pltpu
from jax.sharding import PartitionSpec as P

BS = 64
KB = 32
NP = 16
W = 1024
EARLY = 2
MIB = 1 << 20
Y_GROUPS = [list(range(8)), list(range(8, 16))]


def spread(mask, width):
    count = mask.shape[0]
    lane = lax.broadcasted_iota(jnp.int32, (count, width), 1) // BS
    entry = lax.broadcasted_iota(jnp.int32, (count, width), 0)
    chosen = jnp.where(lane == entry, 1.0, 0.0).astype(jnp.bfloat16)
    return product(mask.astype(jnp.float32).astype(jnp.bfloat16), chosen)


def load(src, dst, chunk, sem):
    rows = pl.ds(chunk * (src.shape[0] // 8), src.shape[0] // 8)
    return pltpu.make_async_copy(src.at[rows], dst.at[rows], sem)


def prep_a(ids, kdist, mask_a, at, to_y, a_z, wide_a, held_a, in_sems, sems):
    row_id, col_id = ids[0], ids[1]
    a_half = row_id // 8
    for n in range(8):
        load(at, held_a, n, in_sems.at[n]).start()
    wide_a[...] = spread(mask_a[...].T, 2 * W)
    for block in range(KB):
        if block % 4 == 0:
            load(at, held_a, block // 4, in_sems.at[block // 4]).wait()
        gain = wide_a[block:block + 1, :].astype(jnp.bfloat16)
        rows = pl.ds(block * BS, BS)
        held_a[rows, :] = held_a[rows, :] * gain
        pos = kdist[row_id * KB + block]
        slot = (pos % KB - 2 * row_id) * BS
        inner = pl.ds(pl.multiple_of(slot, BS), BS)
        for t in range(2):
            tile = (pos // KB - 2 * col_id - t + 2 * NP) % NP
            cols = pl.ds(t * W, W)
            src = held_a.at[rows, cols]
            near = (tile - 8 * a_half + NP) % NP
            far = (near + 8) % NP
            odd = tile % 2 == 1
            even = tile % 2 == 0
            first = jnp.where(odd, tile // 2 % 4 * 2 + t, near)
            first_row = jnp.where(odd, jnp.where(tile // 8 == a_half, 256, 384), t * 128) + slot

            @pl.when(odd | (near < 8))
            def _():
                dst = to_y.at[first, pl.ds(pl.multiple_of(first_row, BS), BS), :]
                pltpu.make_async_copy(src, dst, sems.at[0]).start()

            @pl.when(even & (near > 0) & (near <= 8))
            def _():
                dst = to_y.at[near - 1, pl.ds(pl.multiple_of(t * 128 + slot, BS), BS), :]
                pltpu.make_async_copy(src, dst, sems.at[0]).start()

            @pl.when(even & (far <= 8))
            def _():
                pltpu.make_async_copy(src, a_z.at[far // 2, inner, cols], sems.at[1]).start()

    for n, ref in enumerate((to_y, a_z)):
        pltpu.make_async_copy(ref, ref, sems.at[n]).wait()


def prep_b(ids, kdist_in, mask_in, bmat, x0, x1, x2, x3, b_early, b_rest,
           kdist, mask_b, wide_b, held_b, in_sems, sems):
    small = [pltpu.make_async_copy(mask_in, mask_b, in_sems.at[8]), pltpu.make_async_copy(kdist_in, kdist, in_sems.at[9])]
    for copy in small:
        copy.start()
    row_id, col_id = ids[0], ids[1]
    b_half, here = col_id // 4, col_id % 4
    to_x = (x0, x1, x2, x3)
    for n in range(8):
        load(bmat, held_b, n, in_sems.at[n]).start()
    for copy in small:
        copy.wait()
    wide_b[...] = spread(mask_b[...], W)
    for block in range(2 * KB):
        if block % 8 == 0:
            load(bmat, held_b, block // 8, in_sems.at[block // 8]).wait()
        gain = wide_b[block:block + 1, :].astype(jnp.bfloat16)
        rows = pl.ds(block * BS, BS)
        held_b[rows, :] = held_b[rows, :] * gain
        pos = kdist[col_id * 2 * KB + block]
        inner = pl.ds(pl.multiple_of((pos % KB - 4 * col_id) * BS, BS), BS)
        tile = (pos // KB - row_id + NP) % NP
        src = held_b.at[rows, :]
        near = (tile - 8 * b_half + NP) % NP
        far = (near + 8) % NP
        odd = tile % 2 == 1
        even = tile % 2 == 0
        first = (jnp.where(odd, tile, near) // 2 - here + 8) % 4
        kind = jnp.where(odd, jnp.where(tile // 8 == b_half, 1, 3), 0)
        second = (near // 2 - 1 - here + 8) % 4

        def send(hop, kind):
            def to(n):
                def run():
                    pltpu.make_async_copy(src, to_x[n].at[kind, inner, :], sems.at[n]).start()

                return run

            lax.cond(hop < 2, lambda: lax.cond(hop == 0, to(0), to(1)), lambda: lax.cond(hop == 2, to(2), to(3)))

        @pl.when(odd | (near < 8))
        def _():
            send(first, kind)

        @pl.when(even & (near > 0) & (near <= 8))
        def _():
            send(second, 2)

        @pl.when(even & (far < 2 * EARLY))
        def _():
            pltpu.make_async_copy(src, b_early.at[far // 2, inner, :], sems.at[4]).start()

        @pl.when(even & (far >= 2 * EARLY) & (far <= 8))
        def _():
            pltpu.make_async_copy(src, b_rest.at[far // 2 - EARLY, inner, :], sems.at[5]).start()

    for n, ref in enumerate((x0, x1, x2, x3, b_early, b_rest)):
        pltpu.make_async_copy(ref, ref, sems.at[n]).wait()


CONTRACT = (((0,), (0,)), ((), ()))


def product(left, right):
    return lax.dot_general(left, right, CONTRACT, preferred_element_type=jnp.float32)


def multiply(ids, near_a, e_far, o_near, o_cross, o_swap, r0, r1, r2, r3, p0, p1, p2, p3,
             out, left_out, left_v, b_v, sems, out_sem):
    row_id, col_id = ids[0], ids[1]
    core = row_id % 2
    a_half = row_id // 8
    b_half, here = col_id // 4, col_id % 4
    copies = []

    def fetch(src, dst):
        copy = pltpu.make_async_copy(src, dst, sems.at[len(copies)])
        copy.start()
        copies.append(copy)

    def group(which):
        return pl.ds(pl.multiple_of(which * W, W), W)

    sources = pl.ds(0, 8)
    a_near = pl.ds(pl.multiple_of(a_half * 8, 8), 8)
    a_far = pl.ds(pl.multiple_of(8 - a_half * 8, 8), 8)
    for hop, near in enumerate((r0, r1, r2, r3)):
        place = (here - hop + 4) % 4
        fetch(near.at[pl.ds(0, 3)], b_v.at[:, pl.ds(pl.multiple_of((b_half * 4 + place) * 256, 256), 256)])
    for hop, far in enumerate((p0, p1, p2, p3)):
        place = (here - hop + 4) % 4
        rows = pl.ds(pl.multiple_of(((1 - b_half) * 4 + place) * 256, 256), 256)
        base = here if hop == 0 else 0
        fetch(far.at[base], b_v.at[0, rows])
        fetch(far.at[base + 1], b_v.at[2, rows])
    fetch(near_a.at[sources, pl.ds(pl.multiple_of(core * 128, 128), 128)], left_v.at[0, core, a_near])
    fetch(e_far.at[sources, :, group(core)], left_v.at[0, core, a_far])
    fetch(near_a.at[sources, pl.ds(256, 128)], left_v.at[1, core, a_near])
    fetch(o_cross, left_v.at[1, core, a_far])
    ready = len(copies)
    fetch(o_near, left_v.at[0, 1 - core, a_near])
    fetch(o_swap, left_v.at[0, 1 - core, a_far])
    fetch(near_a.at[sources, pl.ds(pl.multiple_of(128 - core * 128, 128), 128)], left_v.at[1, 1 - core, a_near])
    fetch(e_far.at[sources, :, group(1 - core)], left_v.at[1, 1 - core, a_far])
    later = []
    near_rows = pl.ds(pl.multiple_of(b_half * W, W), W)
    near_pieces = pl.ds(pl.multiple_of(b_half * 8, 8), 8)
    for turn, t in enumerate((core, 1 - core)):
        for copy in copies[turn * ready:ready + turn * 4]:
            copy.wait()
        for hop in range(4):
            place = (here - hop + 4) % 4
            part = pltpu.make_async_copy(
                left_v.at[1, t, pl.ds((1 - b_half) * 8 + place * 2, 2)],
                left_out.at[t, pl.ds(hop * 2, 2)], out_sem.at[turn * 4 + hop])
            part.start()
            later.append(part)
        for m in range(4):
            cols = slice(m * 256, (m + 1) * 256)
            total = product(left_v[0, t, :, :, cols].reshape(2 * W, 256), b_v[2 * t])
            total += product(left_v[1, t, near_pieces, :, cols].reshape(W, 256), b_v[1, near_rows])
            out[pl.ds(pl.multiple_of(t * W + m * 256, 256), 256), :] = total
    for part in later:
        part.wait()


def finish(filt, part, left, right, out, wide, done, sems):
    wide[...] = spread(filt[...], W)
    copies = []
    for t in range(2):
        for m in range(4):
            first = t * W + m * 256
            if len(copies) >= 2:
                copies[-2].wait()
            spot = done.at[len(copies) % 2]
            total = product(left[t, :, :, m * 256:(m + 1) * 256].reshape(W, 256), right[...].reshape(W, W))
            total += part[first:first + 256, :]
            for i in range(4):
                rows = slice(i * BS, (i + 1) * BS)
                block = first // BS + i
                spot[rows, :] = total[rows, :] * wide[block:block + 1, :]
            copies.append(pltpu.make_async_copy(spot, out.at[pl.ds(first, 256)], sems.at[len(copies) % 2]))
            copies[-1].start()
    for copy in copies[-2:]:
        copy.wait()


SMEM = pl.BlockSpec(memory_space=pltpu.SMEM)
ANY = pl.BlockSpec(memory_space=pl.ANY)
HBM = pl.BlockSpec(memory_space=pltpu.HBM)
VMEM = pl.BlockSpec(memory_space=pltpu.VMEM)


def bf16(*shape):
    return pltpu.HBM(shape, jnp.bfloat16)


def in_hbm(*values):
    return [pltpu.with_memory_space_constraint(value, pltpu.HBM) for value in values]


def in_vmem(*values):
    return [pltpu.with_memory_space_constraint(value, pltpu.VMEM) for value in values]


def on_device(at, bmat, mask_a, mask_b, filt, kdist):
    row_id = lax.axis_index("row")
    col_id = lax.axis_index("col")
    ids = jnp.stack([row_id, col_id]).astype(jnp.int32)
    here = col_id % 4

    def swap_z_hi(value):
        return lax.ppermute(value, "row", [(i, i ^ 8) for i in range(16)])

    def swap_z_lo(value):
        return lax.ppermute(value, "col", [(i, i ^ 4) for i in range(8)])

    def swap_core(value):
        return lax.ppermute(value, "row", [(i, i ^ 1) for i in range(16)])

    def along_x(value, hop):
        return lax.ppermute(value, "col", [(i, i // 4 * 4 + (i % 4 + hop) % 4) for i in range(8)])

    def along_y(value):
        return lax.all_to_all(value, "row", 0, 0, axis_index_groups=Y_GROUPS, tiled=True)

    x0, x1, x2, x3, b_early, b_rest = pl.pallas_call(
        prep_b,
        out_shape=[bf16(4, 256, W)] * 4 + [bf16(EARLY, 256, W), bf16(5 - EARLY, 256, W)],
        in_specs=[SMEM, HBM, HBM, HBM],
        out_specs=[HBM] * 6,
        scratch_shapes=[pltpu.SMEM((512,), jnp.int32), pltpu.VMEM((16, 64), jnp.int32),
                        pltpu.VMEM((64, W), jnp.float32), pltpu.VMEM((4096, W), jnp.bfloat16),
                        pltpu.SemaphoreType.DMA((10,)), pltpu.SemaphoreType.DMA((6,))],
        compiler_params=pltpu.CompilerParams(vmem_limit_bytes=24 * MIB),
        name="prep_b",
    )(ids, *in_hbm(kdist, mask_b.T, bmat))

    at, b_early = lax.optimization_barrier((at, b_early))
    a_y, a_z = pl.pallas_call(
        prep_a,
        out_shape=[bf16(8, 512, W), bf16(5, 128, 2 * W)],
        in_specs=[SMEM, SMEM, VMEM, HBM],
        out_specs=[HBM] * 2,
        scratch_shapes=[pltpu.VMEM((32, 2 * W), jnp.float32), pltpu.VMEM((2048, 2 * W), jnp.bfloat16),
                        pltpu.SemaphoreType.DMA((8,)), pltpu.SemaphoreType.DMA((2,))],
        compiler_params=pltpu.CompilerParams(vmem_limit_bytes=24 * MIB),
        name="prep_a",
    )(ids, kdist, mask_a, *in_hbm(at))

    early = swap_z_lo(b_early)
    a_y, a_z, early = lax.optimization_barrier((a_y, a_z, early))
    near_a = along_y(a_y)
    a_cross = swap_z_hi(a_z)
    r1, r3 = along_x(x1, 1), along_x(x3, 3)
    x2, r1, r3 = lax.optimization_barrier((x2, r1, r3))
    r2 = along_x(x2, 2)
    b_cross = jnp.concatenate([early, swap_z_lo(b_rest)], axis=0)

    o_send = near_a[:, 384:]
    q_send = jnp.concatenate([v[3:4] for v in (x0, r1, r2, r3)], axis=0)
    a_cross, b_cross, near_a, o_send, q_send = lax.optimization_barrier((a_cross, b_cross, near_a, o_send, q_send))
    o_cross = swap_z_hi(o_send)
    o_near = swap_core(near_a[:, 256:384])

    e_far = along_y(jnp.stack([a_cross[:4], a_cross[1:]], axis=1).reshape(8, 128, 2 * W))
    far = [lax.dynamic_slice_in_dim(b_cross, (here + hop) % 4, 2, 0) for hop in range(1, 4)]
    p1, p3 = along_x(far[0], 1), along_x(far[2], 3)
    p2_send, p1, p3 = lax.optimization_barrier((far[1], p1, p3))
    p2 = along_x(p2_send, 2)

    q_send, o_cross, p1, p3 = lax.optimization_barrier((q_send, o_cross, p1, p3))
    q = swap_z_lo(q_send)
    o_swap = swap_core(o_cross)

    part, left = pl.pallas_call(
        multiply,
        out_shape=[pltpu.VMEM((2 * W, W), jnp.float32), pltpu.VMEM((2, 8, 128, W), jnp.bfloat16)],
        in_specs=[SMEM] + [ANY] * 13,
        out_specs=[VMEM, VMEM],
        scratch_shapes=[pltpu.VMEM((2, 2, 16, 128, W), jnp.bfloat16), pltpu.VMEM((3, 2048, W), jnp.bfloat16),
                        pltpu.SemaphoreType.DMA((20,)), pltpu.SemaphoreType.DMA((8,))],
        compiler_params=pltpu.CompilerParams(vmem_limit_bytes=38 * MIB),
        name="multiply",
    )(ids, *in_hbm(near_a, e_far, o_near, o_cross, o_swap, x0, r1, r2, r3, b_cross, p1, p2, p3))
    return pl.pallas_call(
        finish,
        out_shape=jax.ShapeDtypeStruct((2 * W, W), jnp.float32),
        in_specs=[VMEM] * 4,
        out_specs=HBM,
        scratch_shapes=[pltpu.VMEM((32, W), jnp.float32), pltpu.VMEM((2, 256, W), jnp.float32),
                        pltpu.SemaphoreType.DMA((2,))],
        compiler_params=pltpu.CompilerParams(vmem_limit_bytes=8 * MIB),
        name="finish",
    )(filt.T, *in_vmem(part, left, q))


def solution(mesh):
    in_specs = (
        P("row", "col"),
        P("col", "row"),
        P("row", "col"),
        P("col", "row"),
        P("col", "row"),
        P(),
    )
    out_specs = P("col", "row")
    return jax.shard_map(
        on_device, mesh=mesh, in_specs=in_specs, out_specs=out_specs, check_vma=False
    )
```

```python
import jax
import jax.numpy as jnp
from jax import lax
from jax.experimental import pallas as pl
from jax.experimental.pallas import tpu as pltpu
from jax.sharding import PartitionSpec as P

BS = 64
KB = 32
NP = 16
W = 1024
EARLY = 1
MIB = 1 << 20
Y_GROUPS = [list(range(8)), list(range(8, 16))]


def spread(mask, width):
    count = mask.shape[0]
    lane = lax.broadcasted_iota(jnp.int32, (count, width), 1) // BS
    entry = lax.broadcasted_iota(jnp.int32, (count, width), 0)
    chosen = jnp.where(lane == entry, 1.0, 0.0).astype(jnp.bfloat16)
    return product(mask.astype(jnp.float32).astype(jnp.bfloat16), chosen)


def load(src, dst, chunk, sem):
    rows = pl.ds(chunk * (src.shape[0] // 8), src.shape[0] // 8)
    return pltpu.make_async_copy(src.at[rows], dst.at[rows], sem)


def prep_a(ids, kdist, mask_a, at, to_y, a_z, wide_a, held_a, in_sems, sems):
    row_id, col_id = ids[0], ids[1]
    a_half = row_id // 8
    for n in range(8):
        load(at, held_a, n, in_sems.at[n]).start()
    wide_a[...] = spread(mask_a[...].T, 2 * W)
    for block in range(KB):
        if block % 4 == 0:
            load(at, held_a, block // 4, in_sems.at[block // 4]).wait()
        gain = wide_a[block:block + 1, :].astype(jnp.bfloat16)
        rows = pl.ds(block * BS, BS)
        held_a[rows, :] = held_a[rows, :] * gain
        pos = kdist[row_id * KB + block]
        slot = (pos % KB - 2 * row_id) * BS
        inner = pl.ds(pl.multiple_of(slot, BS), BS)
        for t in range(2):
            tile = (pos // KB - 2 * col_id - t + 2 * NP) % NP
            cols = pl.ds(t * W, W)
            src = held_a.at[rows, cols]
            near = (tile - 8 * a_half + NP) % NP
            far = (near + 8) % NP
            odd = tile % 2 == 1
            even = tile % 2 == 0
            first = jnp.where(odd, tile // 2 % 4 * 2 + t, near)
            first_row = jnp.where(odd, jnp.where(tile // 8 == a_half, 256, 384), t * 128) + slot

            @pl.when(odd | (near < 8))
            def _():
                dst = to_y.at[first, pl.ds(pl.multiple_of(first_row, BS), BS), :]
                pltpu.make_async_copy(src, dst, sems.at[0]).start()

            @pl.when(even & (near > 0) & (near <= 8))
            def _():
                dst = to_y.at[near - 1, pl.ds(pl.multiple_of(t * 128 + slot, BS), BS), :]
                pltpu.make_async_copy(src, dst, sems.at[0]).start()

            @pl.when(even & (far <= 8))
            def _():
                pltpu.make_async_copy(src, a_z.at[far // 2, inner, cols], sems.at[1]).start()

    for n, ref in enumerate((to_y, a_z)):
        pltpu.make_async_copy(ref, ref, sems.at[n]).wait()


def prep_b(ids, kdist_in, mask_in, bmat, x0, x1, x2, x3, b_early, b_rest,
           kdist, mask_b, wide_b, held_b, in_sems, sems):
    small = [pltpu.make_async_copy(mask_in, mask_b, in_sems.at[8]), pltpu.make_async_copy(kdist_in, kdist, in_sems.at[9])]
    for copy in small:
        copy.start()
    row_id, col_id = ids[0], ids[1]
    b_half, here = col_id // 4, col_id % 4
    to_x = (x0, x1, x2, x3)
    for n in range(8):
        load(bmat, held_b, n, in_sems.at[n]).start()
    for copy in small:
        copy.wait()
    wide_b[...] = spread(mask_b[...], W)
    for block in range(2 * KB):
        if block % 8 == 0:
            load(bmat, held_b, block // 8, in_sems.at[block // 8]).wait()
        gain = wide_b[block:block + 1, :].astype(jnp.bfloat16)
        rows = pl.ds(block * BS, BS)
        held_b[rows, :] = held_b[rows, :] * gain
        pos = kdist[col_id * 2 * KB + block]
        inner = pl.ds(pl.multiple_of((pos % KB - 4 * col_id) * BS, BS), BS)
        tile = (pos // KB - row_id + NP) % NP
        src = held_b.at[rows, :]
        near = (tile - 8 * b_half + NP) % NP
        far = (near + 8) % NP
        odd = tile % 2 == 1
        even = tile % 2 == 0
        first = (jnp.where(odd, tile, near) // 2 - here + 8) % 4
        kind = jnp.where(odd, jnp.where(tile // 8 == b_half, 1, 3), 0)
        second = (near // 2 - 1 - here + 8) % 4

        def send(hop, kind):
            def to(n):
                def run():
                    pltpu.make_async_copy(src, to_x[n].at[kind, inner, :], sems.at[n]).start()

                return run

            lax.cond(hop < 2, lambda: lax.cond(hop == 0, to(0), to(1)), lambda: lax.cond(hop == 2, to(2), to(3)))

        @pl.when(odd | (near < 8))
        def _():
            send(first, kind)

        @pl.when(even & (near > 0) & (near <= 8))
        def _():
            send(second, 2)

        @pl.when(even & (far < 2 * EARLY))
        def _():
            pltpu.make_async_copy(src, b_early.at[far // 2, inner, :], sems.at[4]).start()

        @pl.when(even & (far >= 2 * EARLY) & (far <= 8))
        def _():
            pltpu.make_async_copy(src, b_rest.at[far // 2 - EARLY, inner, :], sems.at[5]).start()

    for n, ref in enumerate((x0, x1, x2, x3, b_early, b_rest)):
        pltpu.make_async_copy(ref, ref, sems.at[n]).wait()


CONTRACT = (((0,), (0,)), ((), ()))


def product(left, right):
    return lax.dot_general(left, right, CONTRACT, preferred_element_type=jnp.float32)


def multiply(ids, near_a, e_far, o_near, o_cross, o_swap, r0, r1, r2, r3, p0, p1, p2, p3,
             out, left_out, left_v, b_v, sems, out_sem):
    row_id, col_id = ids[0], ids[1]
    core = row_id % 2
    a_half = row_id // 8
    b_half, here = col_id // 4, col_id % 4
    copies = []

    def fetch(src, dst):
        copy = pltpu.make_async_copy(src, dst, sems.at[len(copies)])
        copy.start()
        copies.append(copy)

    def group(which):
        return pl.ds(pl.multiple_of(which * W, W), W)

    sources = pl.ds(0, 8)
    a_near = pl.ds(pl.multiple_of(a_half * 8, 8), 8)
    a_far = pl.ds(pl.multiple_of(8 - a_half * 8, 8), 8)
    for hop, near in enumerate((r0, r1, r2, r3)):
        place = (here - hop + 4) % 4
        fetch(near.at[pl.ds(0, 3)], b_v.at[:, pl.ds(pl.multiple_of((b_half * 4 + place) * 256, 256), 256)])
    for hop, far in enumerate((p0, p1, p2, p3)):
        place = (here - hop + 4) % 4
        rows = pl.ds(pl.multiple_of(((1 - b_half) * 4 + place) * 256, 256), 256)
        base = here if hop == 0 else 0
        fetch(far.at[base], b_v.at[0, rows])
        fetch(far.at[base + 1], b_v.at[2, rows])
    fetch(near_a.at[sources, pl.ds(pl.multiple_of(core * 128, 128), 128)], left_v.at[0, core, a_near])
    fetch(e_far.at[sources, :, group(core)], left_v.at[0, core, a_far])
    fetch(near_a.at[sources, pl.ds(256, 128)], left_v.at[1, core, a_near])
    fetch(o_cross, left_v.at[1, core, a_far])
    ready = len(copies)
    fetch(o_near, left_v.at[0, 1 - core, a_near])
    fetch(o_swap, left_v.at[0, 1 - core, a_far])
    fetch(near_a.at[sources, pl.ds(pl.multiple_of(128 - core * 128, 128), 128)], left_v.at[1, 1 - core, a_near])
    fetch(e_far.at[sources, :, group(1 - core)], left_v.at[1, 1 - core, a_far])
    later = []
    near_rows = pl.ds(pl.multiple_of(b_half * W, W), W)
    near_pieces = pl.ds(pl.multiple_of(b_half * 8, 8), 8)
    for turn, t in enumerate((core, 1 - core)):
        for copy in copies[turn * ready:ready + turn * 4]:
            copy.wait()
        for hop in range(4):
            place = (here - hop + 4) % 4
            part = pltpu.make_async_copy(
                left_v.at[1, t, pl.ds((1 - b_half) * 8 + place * 2, 2)],
                left_out.at[t, pl.ds(hop * 2, 2)], out_sem.at[turn * 4 + hop])
            part.start()
            later.append(part)
        for m in range(4):
            cols = slice(m * 256, (m + 1) * 256)
            total = product(left_v[0, t, :, :, cols].reshape(2 * W, 256), b_v[2 * t])
            total += product(left_v[1, t, near_pieces, :, cols].reshape(W, 256), b_v[1, near_rows])
            out[pl.ds(pl.multiple_of(t * W + m * 256, 256), 256), :] = total
    for part in later:
        part.wait()


def finish(filt, part, left, right, out, wide, done, sems):
    wide[...] = spread(filt[...], W)
    copies = []
    for t in range(2):
        for m in range(4):
            first = t * W + m * 256
            if len(copies) >= 2:
                copies[-2].wait()
            spot = done.at[len(copies) % 2]
            total = product(left[t, :, :, m * 256:(m + 1) * 256].reshape(W, 256), right[...].reshape(W, W))
            total += part[first:first + 256, :]
            for i in range(4):
                rows = slice(i * BS, (i + 1) * BS)
                block = first // BS + i
                spot[rows, :] = total[rows, :] * wide[block:block + 1, :]
            copies.append(pltpu.make_async_copy(spot, out.at[pl.ds(first, 256)], sems.at[len(copies) % 2]))
            copies[-1].start()
    for copy in copies[-2:]:
        copy.wait()


SMEM = pl.BlockSpec(memory_space=pltpu.SMEM)
ANY = pl.BlockSpec(memory_space=pl.ANY)
HBM = pl.BlockSpec(memory_space=pltpu.HBM)
VMEM = pl.BlockSpec(memory_space=pltpu.VMEM)


def bf16(*shape):
    return pltpu.HBM(shape, jnp.bfloat16)


def in_hbm(*values):
    return [pltpu.with_memory_space_constraint(value, pltpu.HBM) for value in values]


def in_vmem(*values):
    return [pltpu.with_memory_space_constraint(value, pltpu.VMEM) for value in values]


def on_device(at, bmat, mask_a, mask_b, filt, kdist):
    row_id = lax.axis_index("row")
    col_id = lax.axis_index("col")
    ids = jnp.stack([row_id, col_id]).astype(jnp.int32)
    here = col_id % 4

    def swap_z_hi(value):
        return lax.ppermute(value, "row", [(i, i ^ 8) for i in range(16)])

    def swap_z_lo(value):
        return lax.ppermute(value, "col", [(i, i ^ 4) for i in range(8)])

    def swap_core(value):
        return lax.ppermute(value, "row", [(i, i ^ 1) for i in range(16)])

    def along_x(value, hop):
        return lax.ppermute(value, "col", [(i, i // 4 * 4 + (i % 4 + hop) % 4) for i in range(8)])

    def along_y(value):
        return lax.all_to_all(value, "row", 0, 0, axis_index_groups=Y_GROUPS, tiled=True)

    x0, x1, x2, x3, b_early, b_rest = pl.pallas_call(
        prep_b,
        out_shape=[bf16(4, 256, W)] * 4 + [bf16(EARLY, 256, W), bf16(5 - EARLY, 256, W)],
        in_specs=[SMEM, HBM, HBM, HBM],
        out_specs=[HBM] * 6,
        scratch_shapes=[pltpu.SMEM((512,), jnp.int32), pltpu.VMEM((16, 64), jnp.int32),
                        pltpu.VMEM((64, W), jnp.float32), pltpu.VMEM((4096, W), jnp.bfloat16),
                        pltpu.SemaphoreType.DMA((10,)), pltpu.SemaphoreType.DMA((6,))],
        compiler_params=pltpu.CompilerParams(vmem_limit_bytes=24 * MIB),
        name="prep_b",
    )(ids, *in_hbm(kdist, mask_b.T, bmat))

    at, b_early = lax.optimization_barrier((at, b_early))
    a_y, a_z = pl.pallas_call(
        prep_a,
        out_shape=[bf16(8, 512, W), bf16(5, 128, 2 * W)],
        in_specs=[SMEM, SMEM, VMEM, HBM],
        out_specs=[HBM] * 2,
        scratch_shapes=[pltpu.VMEM((32, 2 * W), jnp.float32), pltpu.VMEM((2048, 2 * W), jnp.bfloat16),
                        pltpu.SemaphoreType.DMA((8,)), pltpu.SemaphoreType.DMA((2,))],
        compiler_params=pltpu.CompilerParams(vmem_limit_bytes=24 * MIB),
        name="prep_a",
    )(ids, kdist, mask_a, *in_hbm(at))

    early = swap_z_lo(b_early)
    a_y, a_z, early = lax.optimization_barrier((a_y, a_z, early))
    near_a = along_y(a_y)
    a_cross = swap_z_hi(a_z)
    r1, r3 = along_x(x1, 1), along_x(x3, 3)
    x2, r1, r3 = lax.optimization_barrier((x2, r1, r3))
    r2 = along_x(x2, 2)
    b_cross = jnp.concatenate([early, swap_z_lo(b_rest)], axis=0)

    o_send = near_a[:, 384:]
    q_send = jnp.concatenate([v[3:4] for v in (x0, r1, r2, r3)], axis=0)
    a_cross, near_a, o_send, q_send = lax.optimization_barrier((a_cross, near_a, o_send, q_send))
    o_cross = swap_z_hi(o_send)
    o_near = swap_core(near_a[:, 256:384])

    e_far = along_y(jnp.stack([a_cross[:4], a_cross[1:]], axis=1).reshape(8, 128, 2 * W))
    far = [lax.dynamic_slice_in_dim(b_cross, (here + hop) % 4, 2, 0) for hop in range(1, 4)]
    p1, p3 = along_x(far[0], 1), along_x(far[2], 3)
    p2_send, p1, p3 = lax.optimization_barrier((far[1], p1, p3))
    p2 = along_x(p2_send, 2)

    q_send, o_cross, p1, p3 = lax.optimization_barrier((q_send, o_cross, p1, p3))
    q = swap_z_lo(q_send)
    o_swap = swap_core(o_cross)

    part, left = pl.pallas_call(
        multiply,
        out_shape=[pltpu.VMEM((2 * W, W), jnp.float32), pltpu.VMEM((2, 8, 128, W), jnp.bfloat16)],
        in_specs=[SMEM] + [ANY] * 13,
        out_specs=[VMEM, VMEM],
        scratch_shapes=[pltpu.VMEM((2, 2, 16, 128, W), jnp.bfloat16), pltpu.VMEM((3, 2048, W), jnp.bfloat16),
                        pltpu.SemaphoreType.DMA((20,)), pltpu.SemaphoreType.DMA((8,))],
        compiler_params=pltpu.CompilerParams(vmem_limit_bytes=38 * MIB),
        name="multiply",
    )(ids, *in_hbm(near_a, e_far, o_near, o_cross, o_swap, x0, r1, r2, r3, b_cross, p1, p2, p3))
    return pl.pallas_call(
        finish,
        out_shape=jax.ShapeDtypeStruct((2 * W, W), jnp.float32),
        in_specs=[VMEM] * 4,
        out_specs=HBM,
        scratch_shapes=[pltpu.VMEM((32, W), jnp.float32), pltpu.VMEM((2, 256, W), jnp.float32),
                        pltpu.SemaphoreType.DMA((2,))],
        compiler_params=pltpu.CompilerParams(vmem_limit_bytes=8 * MIB),
        name="finish",
    )(filt.T, *in_vmem(part, left, q))


def solution(mesh):
    in_specs = (
        P("row", "col"),
        P("col", "row"),
        P("row", "col"),
        P("col", "row"),
        P("col", "row"),
        P(),
    )
    out_specs = P("col", "row")
    return jax.shard_map(
        on_device, mesh=mesh, in_specs=in_specs, out_specs=out_specs, check_vma=False
    )
```

```python
import jax
import jax.numpy as jnp
from jax import lax
from jax.experimental import pallas as pl
from jax.experimental.pallas import tpu as pltpu
from jax.sharding import PartitionSpec as P

BS = 64
KB = 32
NP = 16
W = 1024
EARLY = 1
MIB = 1 << 20
Y_GROUPS = [list(range(8)), list(range(8, 16))]


def spread(mask, width):
    count = mask.shape[0]
    lane = lax.broadcasted_iota(jnp.int32, (count, width), 1) // BS
    entry = lax.broadcasted_iota(jnp.int32, (count, width), 0)
    chosen = jnp.where(lane == entry, 1.0, 0.0).astype(jnp.bfloat16)
    return product(mask.astype(jnp.float32).astype(jnp.bfloat16), chosen)


def load(src, dst, chunk, sem):
    rows = pl.ds(chunk * (src.shape[0] // 8), src.shape[0] // 8)
    return pltpu.make_async_copy(src.at[rows], dst.at[rows], sem)


def prep_a(ids, kdist, mask_a, at, to_y, a_z, wide_a, held_a, in_sems, sems):
    row_id, col_id = ids[0], ids[1]
    a_half = row_id // 8
    for n in range(8):
        load(at, held_a, n, in_sems.at[n]).start()
    wide_a[...] = spread(mask_a[...].T, 2 * W)
    for block in range(KB):
        if block % 4 == 0:
            load(at, held_a, block // 4, in_sems.at[block // 4]).wait()
        gain = wide_a[block:block + 1, :].astype(jnp.bfloat16)
        rows = pl.ds(block * BS, BS)
        held_a[rows, :] = held_a[rows, :] * gain
        pos = kdist[row_id * KB + block]
        slot = (pos % KB - 2 * row_id) * BS
        inner = pl.ds(pl.multiple_of(slot, BS), BS)
        for t in range(2):
            tile = (pos // KB - 2 * col_id - t + 2 * NP) % NP
            cols = pl.ds(t * W, W)
            src = held_a.at[rows, cols]
            near = (tile - 8 * a_half + NP) % NP
            far = (near + 8) % NP
            odd = tile % 2 == 1
            even = tile % 2 == 0
            first = jnp.where(odd, tile // 2 % 4 * 2 + t, near)
            first_row = jnp.where(odd, jnp.where(tile // 8 == a_half, 256, 384), t * 128) + slot

            @pl.when(odd | (near < 8))
            def _():
                dst = to_y.at[first, pl.ds(pl.multiple_of(first_row, BS), BS), :]
                pltpu.make_async_copy(src, dst, sems.at[0]).start()

            @pl.when(even & (near > 0) & (near <= 8))
            def _():
                dst = to_y.at[near - 1, pl.ds(pl.multiple_of(t * 128 + slot, BS), BS), :]
                pltpu.make_async_copy(src, dst, sems.at[0]).start()

            @pl.when(even & (far <= 8))
            def _():
                pltpu.make_async_copy(src, a_z.at[far // 2, inner, cols], sems.at[1]).start()

    for n, ref in enumerate((to_y, a_z)):
        pltpu.make_async_copy(ref, ref, sems.at[n]).wait()


def prep_b(ids, kdist_in, mask_in, bmat, x0, x1, x2, x3, b_early, b_rest,
           kdist, mask_b, wide_b, held_b, in_sems, sems):
    small = [pltpu.make_async_copy(mask_in, mask_b, in_sems.at[8]), pltpu.make_async_copy(kdist_in, kdist, in_sems.at[9])]
    for copy in small:
        copy.start()
    row_id, col_id = ids[0], ids[1]
    b_half, here = col_id // 4, col_id % 4
    to_x = (x0, x1, x2, x3)
    for n in range(8):
        load(bmat, held_b, n, in_sems.at[n]).start()
    for copy in small:
        copy.wait()
    wide_b[...] = spread(mask_b[...], W)
    for block in range(2 * KB):
        if block % 8 == 0:
            load(bmat, held_b, block // 8, in_sems.at[block // 8]).wait()
        gain = wide_b[block:block + 1, :].astype(jnp.bfloat16)
        rows = pl.ds(block * BS, BS)
        held_b[rows, :] = held_b[rows, :] * gain
        pos = kdist[col_id * 2 * KB + block]
        inner = pl.ds(pl.multiple_of((pos % KB - 4 * col_id) * BS, BS), BS)
        tile = (pos // KB - row_id + NP) % NP
        src = held_b.at[rows, :]
        near = (tile - 8 * b_half + NP) % NP
        far = (near + 8) % NP
        odd = tile % 2 == 1
        even = tile % 2 == 0
        first = (jnp.where(odd, tile, near) // 2 - here + 8) % 4
        kind = jnp.where(odd, jnp.where(tile // 8 == b_half, 1, 3), 0)
        second = (near // 2 - 1 - here + 8) % 4

        def send(hop, kind):
            def to(n):
                def run():
                    pltpu.make_async_copy(src, to_x[n].at[kind, inner, :], sems.at[n]).start()

                return run

            lax.cond(hop < 2, lambda: lax.cond(hop == 0, to(0), to(1)), lambda: lax.cond(hop == 2, to(2), to(3)))

        @pl.when(odd | (near < 8))
        def _():
            send(first, kind)

        @pl.when(even & (near > 0) & (near <= 8))
        def _():
            send(second, 2)

        @pl.when(even & (far < 2 * EARLY))
        def _():
            pltpu.make_async_copy(src, b_early.at[far // 2, inner, :], sems.at[4]).start()

        @pl.when(even & (far >= 2 * EARLY) & (far <= 8))
        def _():
            pltpu.make_async_copy(src, b_rest.at[far // 2 - EARLY, inner, :], sems.at[5]).start()

    for n, ref in enumerate((x0, x1, x2, x3, b_early, b_rest)):
        pltpu.make_async_copy(ref, ref, sems.at[n]).wait()


CONTRACT = (((0,), (0,)), ((), ()))


def product(left, right):
    return lax.dot_general(left, right, CONTRACT, preferred_element_type=jnp.float32)


def multiply(ids, near_a, e_far, o_near, o_cross, o_swap, r0, r1, r2, r3, p0, p1, p2, p3,
             out, left_out, left_v, b_v, sems, out_sem):
    row_id, col_id = ids[0], ids[1]
    core = row_id % 2
    a_half = row_id // 8
    b_half, here = col_id // 4, col_id % 4
    copies = []

    def fetch(src, dst):
        copy = pltpu.make_async_copy(src, dst, sems.at[len(copies)])
        copy.start()
        copies.append(copy)

    def group(which):
        return pl.ds(pl.multiple_of(which * W, W), W)

    sources = pl.ds(0, 8)
    a_near = pl.ds(pl.multiple_of(a_half * 8, 8), 8)
    a_far = pl.ds(pl.multiple_of(8 - a_half * 8, 8), 8)
    for hop, near in enumerate((r0, r1, r2, r3)):
        place = (here - hop + 4) % 4
        fetch(near.at[pl.ds(0, 3)], b_v.at[:, pl.ds(pl.multiple_of((b_half * 4 + place) * 256, 256), 256)])
    for hop, far in enumerate((p0, p1, p2, p3)):
        place = (here - hop + 4) % 4
        rows = pl.ds(pl.multiple_of(((1 - b_half) * 4 + place) * 256, 256), 256)
        base = here if hop == 0 else 0
        fetch(far.at[base], b_v.at[0, rows])
        fetch(far.at[base + 1], b_v.at[2, rows])
    fetch(near_a.at[sources, pl.ds(pl.multiple_of(core * 128, 128), 128)], left_v.at[0, core, a_near])
    fetch(e_far.at[sources, :, group(core)], left_v.at[0, core, a_far])
    fetch(near_a.at[sources, pl.ds(256, 128)], left_v.at[1, core, a_near])
    fetch(o_cross, left_v.at[1, core, a_far])
    ready = len(copies)
    fetch(o_near, left_v.at[0, 1 - core, a_near])
    fetch(o_swap, left_v.at[0, 1 - core, a_far])
    fetch(near_a.at[sources, pl.ds(pl.multiple_of(128 - core * 128, 128), 128)], left_v.at[1, 1 - core, a_near])
    fetch(e_far.at[sources, :, group(1 - core)], left_v.at[1, 1 - core, a_far])
    later = []
    near_rows = pl.ds(pl.multiple_of(b_half * W, W), W)
    near_pieces = pl.ds(pl.multiple_of(b_half * 8, 8), 8)
    for turn, t in enumerate((core, 1 - core)):
        for copy in copies[turn * ready:ready + turn * 4]:
            copy.wait()
        for hop in range(4):
            place = (here - hop + 4) % 4
            part = pltpu.make_async_copy(
                left_v.at[1, t, pl.ds((1 - b_half) * 8 + place * 2, 2)],
                left_out.at[t, pl.ds(hop * 2, 2)], out_sem.at[turn * 4 + hop])
            part.start()
            later.append(part)
        for m in range(4):
            cols = slice(m * 256, (m + 1) * 256)
            total = product(left_v[0, t, :, :, cols].reshape(2 * W, 256), b_v[2 * t])
            total += product(left_v[1, t, near_pieces, :, cols].reshape(W, 256), b_v[1, near_rows])
            out[pl.ds(pl.multiple_of(t * W + m * 256, 256), 256), :] = total
    for part in later:
        part.wait()


def finish(filt, part, left, right, out, wide, done, sems):
    wide[...] = spread(filt[...], W)
    copies = []
    for t in range(2):
        for m in range(4):
            first = t * W + m * 256
            spot = done.at[len(copies)]
            total = product(left[t, :, :, m * 256:(m + 1) * 256].reshape(W, 256), right[...].reshape(W, W))
            total += part[first:first + 256, :]
            for i in range(4):
                rows = slice(i * BS, (i + 1) * BS)
                block = first // BS + i
                spot[rows, :] = total[rows, :] * wide[block:block + 1, :]
            copies.append(pltpu.make_async_copy(spot, out.at[pl.ds(first, 256)], sems.at[len(copies)]))
            copies[-1].start()
    for copy in copies:
        copy.wait()


SMEM = pl.BlockSpec(memory_space=pltpu.SMEM)
ANY = pl.BlockSpec(memory_space=pl.ANY)
HBM = pl.BlockSpec(memory_space=pltpu.HBM)
VMEM = pl.BlockSpec(memory_space=pltpu.VMEM)


def bf16(*shape):
    return pltpu.HBM(shape, jnp.bfloat16)


def in_hbm(*values):
    return [pltpu.with_memory_space_constraint(value, pltpu.HBM) for value in values]


def in_vmem(*values):
    return [pltpu.with_memory_space_constraint(value, pltpu.VMEM) for value in values]


def on_device(at, bmat, mask_a, mask_b, filt, kdist):
    row_id = lax.axis_index("row")
    col_id = lax.axis_index("col")
    ids = jnp.stack([row_id, col_id]).astype(jnp.int32)
    here = col_id % 4

    def swap_z_hi(value):
        return lax.ppermute(value, "row", [(i, i ^ 8) for i in range(16)])

    def swap_z_lo(value):
        return lax.ppermute(value, "col", [(i, i ^ 4) for i in range(8)])

    def swap_core(value):
        return lax.ppermute(value, "row", [(i, i ^ 1) for i in range(16)])

    def along_x(value, hop):
        return lax.ppermute(value, "col", [(i, i // 4 * 4 + (i % 4 + hop) % 4) for i in range(8)])

    def along_y(value):
        return lax.all_to_all(value, "row", 0, 0, axis_index_groups=Y_GROUPS, tiled=True)

    x0, x1, x2, x3, b_early, b_rest = pl.pallas_call(
        prep_b,
        out_shape=[bf16(4, 256, W)] * 4 + [bf16(EARLY, 256, W), bf16(5 - EARLY, 256, W)],
        in_specs=[SMEM, HBM, HBM, HBM],
        out_specs=[HBM] * 6,
        scratch_shapes=[pltpu.SMEM((512,), jnp.int32), pltpu.VMEM((16, 64), jnp.int32),
                        pltpu.VMEM((64, W), jnp.float32), pltpu.VMEM((4096, W), jnp.bfloat16),
                        pltpu.SemaphoreType.DMA((10,)), pltpu.SemaphoreType.DMA((6,))],
        compiler_params=pltpu.CompilerParams(vmem_limit_bytes=24 * MIB),
        name="prep_b",
    )(ids, *in_hbm(kdist, mask_b.T, bmat))

    at, b_early = lax.optimization_barrier((at, b_early))
    a_y, a_z = pl.pallas_call(
        prep_a,
        out_shape=[bf16(8, 512, W), bf16(5, 128, 2 * W)],
        in_specs=[SMEM, SMEM, VMEM, HBM],
        out_specs=[HBM] * 2,
        scratch_shapes=[pltpu.VMEM((32, 2 * W), jnp.float32), pltpu.VMEM((2048, 2 * W), jnp.bfloat16),
                        pltpu.SemaphoreType.DMA((8,)), pltpu.SemaphoreType.DMA((2,))],
        compiler_params=pltpu.CompilerParams(vmem_limit_bytes=24 * MIB),
        name="prep_a",
    )(ids, kdist, mask_a, *in_hbm(at))

    early = swap_z_lo(b_early)
    a_y, a_z, early = lax.optimization_barrier((a_y, a_z, early))
    near_a = along_y(a_y)
    a_cross = swap_z_hi(a_z)
    r1, r3 = along_x(x1, 1), along_x(x3, 3)
    x2, r1, r3 = lax.optimization_barrier((x2, r1, r3))
    r2 = along_x(x2, 2)
    b_cross = jnp.concatenate([early, swap_z_lo(b_rest)], axis=0)

    o_send = near_a[:, 384:]
    q_send = jnp.concatenate([v[3:4] for v in (x0, r1, r2, r3)], axis=0)
    a_cross, near_a, o_send, q_send = lax.optimization_barrier((a_cross, near_a, o_send, q_send))
    o_cross = swap_z_hi(o_send)
    o_near = swap_core(near_a[:, 256:384])

    e_far = along_y(jnp.stack([a_cross[:4], a_cross[1:]], axis=1).reshape(8, 128, 2 * W))
    far = [lax.dynamic_slice_in_dim(b_cross, (here + hop) % 4, 2, 0) for hop in range(1, 4)]
    p1, p3 = along_x(far[0], 1), along_x(far[2], 3)
    p2_send, p1, p3 = lax.optimization_barrier((far[1], p1, p3))
    p2 = along_x(p2_send, 2)

    q_send, o_cross, p1, p3 = lax.optimization_barrier((q_send, o_cross, p1, p3))
    q = swap_z_lo(q_send)
    o_swap = swap_core(o_cross)

    part, left = pl.pallas_call(
        multiply,
        out_shape=[pltpu.VMEM((2 * W, W), jnp.float32), pltpu.VMEM((2, 8, 128, W), jnp.bfloat16)],
        in_specs=[SMEM] + [ANY] * 13,
        out_specs=[VMEM, VMEM],
        scratch_shapes=[pltpu.VMEM((2, 2, 16, 128, W), jnp.bfloat16), pltpu.VMEM((3, 2048, W), jnp.bfloat16),
                        pltpu.SemaphoreType.DMA((20,)), pltpu.SemaphoreType.DMA((8,))],
        compiler_params=pltpu.CompilerParams(vmem_limit_bytes=38 * MIB),
        name="multiply",
    )(ids, *in_hbm(near_a, e_far, o_near, o_cross, o_swap, x0, r1, r2, r3, b_cross, p1, p2, p3))
    return pl.pallas_call(
        finish,
        out_shape=jax.ShapeDtypeStruct((2 * W, W), jnp.float32),
        in_specs=[VMEM] * 4,
        out_specs=HBM,
        scratch_shapes=[pltpu.VMEM((32, W), jnp.float32), pltpu.VMEM((8, 256, W), jnp.float32),
                        pltpu.SemaphoreType.DMA((8,))],
        compiler_params=pltpu.CompilerParams(vmem_limit_bytes=16 * MIB),
        name="finish",
    )(filt.T, *in_vmem(part, left, q))


def solution(mesh):
    in_specs = (
        P("row", "col"),
        P("col", "row"),
        P("row", "col"),
        P("col", "row"),
        P("col", "row"),
        P(),
    )
    out_specs = P("col", "row")
    return jax.shard_map(
        on_device, mesh=mesh, in_specs=in_specs, out_specs=out_specs, check_vma=False
    )
```
